1024 devices in a mesh: section: 16 (over z), expert: 64 (over x, y, core).
Axes of the slice: x: 4, y: 8, z: 16, core: 2. Of those that a mesh axis runs over, the one named last changes fastest.
Arguments:
- out_grad: bfloat16 [16, 2048, 2048], P('section', 'expert'), may hold values from -6 to 6
- layer_input: bfloat16 [16, 2048, 2048], P('section', 'expert'), may hold values from -6 to 6
- router_weight: bfloat16 [16, 2048, 64], P('section'), may hold values from -0.125 to 0.125
- expert_ids: int32 [16, 2048, 8], P('section', 'expert'), may hold values from 0 to 63, all different within a row; in each aligned block of 32 rows (0 to 31, 32 to 63, ..., all dimensions but the last counted through in order) at most 6 rows name the same one
- hidden_act: bfloat16 [16, 64, 384, 384], P('section', 'expert'), may hold values from -6 to 6
- down_weight: bfloat16 [16, 64, 384, 2048], P('section', 'expert'), may hold values from -0.3125 to 0.3125
Outputs:
- sent_grad: bfloat16 [16, 2048, 2048], P('section', 'expert')
- hidden_grad: bfloat16 [16, 64, 384, 384], P('section', 'expert')
- router_grad: float32 [16, 2048, 64], P('section', 'expert')
The draws below stay inside these ranges and needn't reach their ends.
Inputs may be any that keep to these rules, and one draw needn't show every extreme that they name: `expert_ids`: each token names 8 different experts. In each aligned block of 32 tokens (the tokens of one device) no expert is named by more than 6 tokens, a bound that some block reaches.
All inputs are finite; a program needn't handle non-finite values.
Results may differ from the reference program's by a relative error of at most 0.0095.
Values may be sent and summed in bfloat16 or wider, within the bound.
No kernel may reach another device: no remote copies, remote signals or barrier semaphores. Data moves between devices by JAX's collectives and lax.ppermute only.
A program may use at most 32 MiB of HBM per device.

```python
import math
import jax
import jax.numpy as jnp
import numpy as np
from jax import lax

D = 2048
F = 384
TOPK = 8
TOK_DEV = 32
SECTIONS = 16
EXPERTS = 64
TOKENS = 2048
CAP = 6
SLOTS = 384
N_EXPERT = 64


def shard_levels(rng, extent, shards, least, high):
    def one(dim, blocks):
        heights = jax.random.uniform(jax.random.fold_in(jax.random.fold_in(rng, 6), dim), (blocks,), jnp.float32, least / len(shards), high / len(shards))
        return jnp.repeat(jnp.exp(heights), extent[dim] // blocks).reshape((-1,) + (1,) * (len(extent) - dim - 1))

    loudness = one(*shards[0])
    for cut in shards[1:]:
        loudness = loudness * one(*cut)
    return loudness


def assign_block(stream_key, own, number, rows, number_of, top, most, lean):
    ranking = jax.random.permutation(stream_key, number_of)
    crowded, common = portions_of(number_of, rows * top, most, lean, True), portions_of(number_of, rows * top, most, lean, False)
    places = jnp.arange(number_of)

    def named(sizes, rotation):
        used = int((sizes > 0).sum())
        fixed = max(1, used // 4)
        passed = fixed + (places - fixed + rotation * (used - fixed)) % max(1, number_of - fixed)
        return jnp.zeros((number_of,), jnp.int32).at[ranking[jnp.where(places < fixed, places, passed)]].set(jnp.asarray(sizes, jnp.int32))

    sizes = jnp.where(number % 4 == 0, named(crowded, number // 4), named(common, number - number // 4 - 1))
    mixed = jax.random.permutation(jax.random.fold_in(own, 3), number_of)
    giver, taker = mixed[0:number_of // 2 * 2:2], mixed[1:number_of // 2 * 2:2]
    margin = jnp.minimum(sizes[giver] - 1, most - sizes[taker]) // 2
    margin = jnp.where((giver == ranking[0]) | (taker == ranking[0]) | (sizes[taker] == 0), 0, jnp.maximum(margin, 0))
    passed = jax.random.randint(jax.random.fold_in(own, 4), (number_of // 2,), 0, 1 << 20) % (margin + 1)
    sizes = sizes.at[giver].add(-passed).at[taker].add(passed)
    members = jnp.searchsorted(jnp.cumsum(sizes), jnp.arange(rows * top), side="right").astype(jnp.int32)
    listing = members.reshape(top, rows).T
    listing = listing[jax.random.permutation(jax.random.fold_in(own, 1), rows)]
    rotation = jax.random.randint(jax.random.fold_in(own, 2), (rows, 1), 0, top)
    return jnp.take_along_axis(listing, (jnp.arange(top)[None, :] + rotation) % top, axis=1)


def portions_of(number_of, total, limit, slope, full):
    weights = [(1 << 20) // math.isqrt(grade ** slope) + 1 for grade in range(1, number_of + 1)]
    largest = limit if full else min(limit, max(-(-total // number_of), total * weights[0] // sum(weights)))
    least = 1 if total - largest >= number_of - 1 else 0
    given, rest = [largest] + [least] * (number_of - 1), total - largest - least * (number_of - 1)
    while rest > 0:
        movable = [i for i in range(1, number_of) if given[i] < largest] or [i for i in range(1, number_of) if given[i] < limit]
        pool, remaining = sum([weights[i] for i in movable]), rest
        for i in movable:
            more = min(limit - given[i], max(1, remaining * weights[i] // pool), rest)
            given[i] = given[i] + more
            rest = rest - more
    return np.array(given)


def gaussian(own_key, dims, scale, reach, split=(), kind=jnp.bfloat16):
    level = shard_levels(own_key, dims, split, -0.22, 0.18) if split else 1.0
    values = jax.random.normal(own_key, dims, jnp.float32) * scale * level
    return jnp.minimum(jnp.maximum(values, -reach), reach).astype(kind)


def setup_inputs(seed: int = 0) -> dict:
    keys = jax.random.split(jax.random.key(seed), 7)
    out_grad = gaussian(keys[0], (SECTIONS, TOKENS, D), 1.0, 6.0, ((0, 16), (1, 64)))
    layer_input = gaussian(keys[1], (SECTIONS, TOKENS, D), 1.0, 6.0, ((0, 16), (1, 64)))
    router_weight = gaussian(keys[2], (SECTIONS, D, EXPERTS), D ** -0.5, 0.125, ((0, 16),))
    expert_ids_keys = jax.random.split(jax.random.fold_in(keys[3], 1), SECTIONS * TOKENS // TOK_DEV)
    expert_ids_turns = jax.random.permutation(jax.random.fold_in(keys[3], 3), SECTIONS * TOKENS // TOK_DEV)
    expert_ids = jax.vmap(lambda own, number: assign_block(jax.random.fold_in(keys[3], 2), own, number, TOK_DEV, EXPERTS, TOPK, CAP, 2))(expert_ids_keys, expert_ids_turns).reshape((SECTIONS, TOKENS, TOPK))
    hidden_act = gaussian(keys[4], (SECTIONS, EXPERTS, SLOTS, F), 1.0, 6.0, ((0, 16), (1, 64)))
    down_weight = gaussian(keys[5], (SECTIONS, EXPERTS, F, D), F ** -0.5, 0.3125, ((0, 16), (1, 64)))
    return {"out_grad": out_grad, "layer_input": layer_input, "router_weight": router_weight, "expert_ids": expert_ids, "hidden_act": hidden_act, "down_weight": down_weight}


def expert_pass(operands):
    hidden, w_down, dispatched, slot_gates = operands
    expert_out = jnp.dot(hidden, w_down, preferred_element_type=jnp.float32)
    slot_dg = jnp.sum(dispatched.astype(jnp.float32) * expert_out, axis=-1)
    scaled = (slot_gates.astype(jnp.float32)[:, None] * dispatched.astype(jnp.float32)).astype(jnp.bfloat16)
    hidden_grad = jnp.dot(scaled, w_down.T, preferred_element_type=jnp.float32).astype(jnp.bfloat16)
    return slot_dg, hidden_grad


def section_backward(out_grads, inputs, router, chosen_ids, hidden, w_down):
    logits = jnp.dot(inputs, router, preferred_element_type=jnp.float32)
    picked = (chosen_ids[:, :, None] == jnp.arange(EXPERTS, dtype=jnp.int32)[None, None, :]).astype(jnp.float32)
    chosen_logits = jnp.sum(picked * logits[:, None, :], axis=-1)
    weights = jnp.exp(chosen_logits)
    gate_vals = (weights / jnp.sum(weights, axis=-1, keepdims=True)).astype(jnp.bfloat16)
    blocked = picked.reshape(N_EXPERT, TOK_DEV * TOPK, EXPERTS)
    before = jnp.cumsum(blocked, axis=1) - blocked
    slot_rank = jnp.sum(before * blocked, axis=-1).astype(jnp.int32).reshape(TOKENS, TOPK)
    source = (jnp.arange(TOKENS, dtype=jnp.int32) // TOK_DEV)[:, None]
    slot_row = (source * CAP + slot_rank).astype(jnp.int32)
    spread = jnp.broadcast_to(out_grads[:, None, :], (TOKENS, TOPK, D))
    dispatched = jnp.zeros((EXPERTS, SLOTS, D), jnp.bfloat16).at[chosen_ids, slot_row].set(spread)
    slot_gates = jnp.zeros((EXPERTS, SLOTS), jnp.bfloat16).at[chosen_ids, slot_row].set(gate_vals)
    slot_dg, hidden_grad = lax.map(expert_pass, (hidden, w_down, dispatched, slot_gates))
    gate_grad = slot_dg[chosen_ids, slot_row]
    gate_float = gate_vals.astype(jnp.float32)
    dchosen = gate_float * (gate_grad - jnp.sum(gate_float * gate_grad, axis=-1, keepdims=True))
    logit_grad = jnp.sum(dchosen[:, :, None] * picked, axis=1).astype(jnp.bfloat16)
    input_grad = (out_grads.astype(jnp.float32) + jnp.dot(logit_grad, router.T, preferred_element_type=jnp.float32)).astype(jnp.bfloat16)
    router_grad = jnp.dot(inputs.T, logit_grad, preferred_element_type=jnp.float32)
    return input_grad, hidden_grad, router_grad


def reference(out_grad, layer_input, router_weight, expert_ids, hidden_act, down_weight):
    input_list = []
    hidden_list = []
    router_list = []
    for section_index in range(SECTIONS):
        input_grad, hidden_grad, router_grad = section_backward(out_grad[section_index], layer_input[section_index], router_weight[section_index], expert_ids[section_index], hidden_act[section_index], down_weight[section_index])
        input_list.append(input_grad)
        hidden_list.append(hidden_grad)
        router_list.append(router_grad)
    input_all = jnp.stack(input_list, axis=0)
    sent_grad = jnp.roll(input_all, -1, axis=0)
    return sent_grad, jnp.stack(hidden_list, axis=0), jnp.stack(router_list, axis=0)
```

```python
import jax
import jax.numpy as jnp
import numpy as np
from jax import lax
from jax.experimental import pallas as pl
from jax.experimental.pallas import tpu as pltpu
from jax.sharding import PartitionSpec as P

F32 = jnp.float32
BF16 = jnp.bfloat16
PEERS = 64
CAP = 6
TOK = 32
WIDE = 256
PARTS = 8
ROWS = PARTS * CAP
CHUNK = ROWS + 8
SLOTS = PEERS * CAP
GROUPS = 16


def dot(a, b, ca, cb):
    return lax.dot_general(a, b, (((ca,), (cb,)), ((), ())), preferred_element_type=F32)


def iota(shape, dim):
    return lax.broadcasted_iota(jnp.int32, shape, dim)


def compaction():
    p = np.zeros((8 * ROWS, 8 * ROWS), np.float32)
    for part in range(PARTS):
        for b in range(8):
            for c in range(CAP):
                p[part * ROWS + b * CAP + c, b * ROWS + part * CAP + c] = 1
    return p


def spreading():
    m = np.zeros((128, CAP * 128), np.float32)
    for piece in range(3):
        for b in range(4):
            for c in range(CAP):
                row = piece * 32 + b * CAP + c
                m[row, c * 128 + b * TOK : c * 128 + (b + 1) * TOK] = 1
    return m


def pack_kernel(og_ref, li_ref, rw_ref, ids_ref, send_ref, gate_ref, code_ref, gt_ref, ct_ref):
    ids = ids_ref[...]
    logits = dot(rw_ref[...], li_ref[...], 1, 1)
    expert = iota((PEERS, TOK), 0)
    named = jnp.zeros((PEERS, TOK), F32)
    for k in range(8):
        named = jnp.where(ids[k : k + 1, :] == expert, 1.0, named)
    weights = jnp.where(named > 0.5, jnp.exp(logits), 0.0)
    gates = (weights / jnp.sum(weights, axis=0, keepdims=True)).astype(BF16)
    token = iota((TOK, WIDE), 0)
    lane = iota((TOK, WIDE), 1) & (TOK - 1)
    tile = jnp.where(token == lane, 1.0, 0.0).astype(BF16)
    ahead = jnp.where(token < lane, 1.0, 0.0).astype(BF16)
    named_b = named.astype(BF16)
    code = jnp.where(dot(named_b, tile, 1, 0) > 0.5, dot(named_b, ahead, 1, 0), -1.0)
    ct_ref[...] = code
    gt_ref[...] = dot(gates, tile, 1, 0)
    gates_f = gates.astype(F32)
    gate_ref[...] = gates_f
    code_ref[...] = code[:, :TOK]

    choice = iota((8, TOK), 0)
    compact = jnp.zeros((8, TOK), F32)
    for k in range(8):
        one = jnp.sum(jnp.where(ids[k : k + 1, :] == expert, gates_f, 0.0), axis=0, keepdims=True)
        compact = jnp.where(choice == k, one, compact)
    t128, l128 = iota((TOK, 128), 0), iota((TOK, 128), 1)
    put_ids = jnp.where(t128 == l128, 1.0, 0.0).astype(BF16)
    put_gates = jnp.where(t128 + TOK == l128, 1.0, 0.0).astype(BF16)
    info = dot(ids.astype(F32).astype(BF16), put_ids, 1, 0) + dot(
        compact.astype(BF16), put_gates, 1, 0
    )
    send_ref[:, ROWS:, 128:] = jnp.broadcast_to(info.astype(BF16)[None], (PEERS, 8, 128))

    spread = dot(li_ref[...], tile[:, :128], 0, 0).reshape(PEERS, 4, 8, 128)
    quarter = iota((PEERS, 8, 128), 2) // TOK
    columns = spread[:, 0]
    for h in range(1, 4):
        columns = jnp.where(quarter == h, spread[:, h], columns)
    send_ref[:, ROWS:, :128] = columns.astype(BF16)

    stacked = jnp.concatenate(
        [og_ref[:, j * WIDE : (j + 1) * WIDE] for j in range(PARTS)], axis=0
    )
    row = iota((ROWS, WIDE), 0)
    part = jnp.zeros((ROWS, WIDE), jnp.int32)
    for j in range(1, PARTS):
        part = part + jnp.where(row >= j * CAP, 1, 0)
    slot = jnp.where(iota((ROWS, WIDE), 1) // TOK == part, row - part * CAP, -2).astype(F32)

    def step(i, carry):
        picks = []
        for u in range(8):
            at = pl.ds(i * 8 + u, 1)
            hit = jnp.broadcast_to(ct_ref[at, :], (ROWS, WIDE)) == slot
            picks.append(
                jnp.where(hit, jnp.broadcast_to(gt_ref[at, :], (ROWS, WIDE)), 0.0).astype(BF16)
            )
        rows = dot(jnp.concatenate(picks, axis=0), stacked, 1, 0).astype(BF16)
        send_ref[pl.ds(i * 8, 8), :ROWS, :] = rows.reshape(8, ROWS, WIDE)
        return carry

    lax.fori_loop(0, PEERS // 8, step, 0)


def expert_kernel(recv_ref, w_ref, h_ref, perm_ref, hg_ref, sdg_ref, rows_ref):
    perm = perm_ref[...]
    for g in range(8):
        chunk = recv_ref[g * 8 : (g + 1) * 8, :, :].reshape(8 * ROWS, WIDE)
        moved = dot(perm, chunk, 1, 0).astype(BF16)
        for j in range(PARTS):
            rows_ref[g * ROWS : (g + 1) * ROWS, j * WIDE : (j + 1) * WIDE] = moved[
                j * ROWS : (j + 1) * ROWS
            ]
    grad = dot(rows_ref[...], w_ref[...], 1, 1)
    hg_ref[...] = grad.astype(BF16)
    prod = grad * h_ref[...].astype(F32)
    part = prod[:, :128] + prod[:, 128:256] + prod[:, 256:]
    gap = jnp.zeros((8, 128), F32)
    pieces = []
    for g in range(GROUPS):
        pieces += [part[g * 24 : (g + 1) * 24], gap]
    padded = jnp.concatenate(pieces, axis=0)
    line = jnp.sum(padded.T, axis=0, keepdims=True)
    which = iota((8, 128), 0) & 3
    out = jnp.zeros((8, 128), F32)
    for t in range(4):
        out = jnp.where(which == t, line[:, t * 128 : (t + 1) * 128], out)
    sdg_ref[...] = jnp.broadcast_to(out[None], (PEERS // 2, 8, 128)).reshape(PEERS * 4, 128)


def side_kernel(ext_ref, sdg_ref, gate_ref, code_ref, cols_ref, ready_ref):
    ready_ref[...] = sdg_ref[...]
    expert = iota((PEERS, 128), 0).astype(F32)
    row, col = iota((128, 128), 0), iota((128, 128), 1)
    ahead = jnp.where((row // TOK == col // TOK) & (row < col), 1.0, 0.0).astype(BF16)
    quarter = iota((8, 128), 1) // TOK

    def gather(blocks, at):
        out = None
        for i, block in enumerate(blocks):
            shift = (i - at) * TOK % 128
            moved = pltpu.roll(block, shift, axis=1) if shift else block
            out = moved if out is None else jnp.where(quarter == i, moved, out)
        return out

    for g in range(GROUPS):
        info = [ext_ref[4 * g + i, :, 128:].astype(F32) for i in range(4)]
        ids, gates = gather(info, 0), gather(info, 1)
        named = jnp.zeros((PEERS, 128), F32)
        dense = jnp.zeros((PEERS, 128), F32)
        for k in range(8):
            hit = ids[k : k + 1, :] == expert
            named = jnp.where(hit, 1.0, named)
            dense = jnp.where(hit, gates[k : k + 1, :], dense)
        rank = dot(named.astype(BF16), ahead, 1, 0)
        code_ref[g] = jnp.where(named > 0.5, rank, -1.0)
        gate_ref[g] = dense
        cols = [ext_ref[4 * g + i, :, :128].astype(F32) for i in range(4)]
        for h in range(4):
            cols_ref[h * 8 : (h + 1) * 8, g * 128 : (g + 1) * 128] = gather(cols, h)


def input_kernel(me_ref, s_ref, code_ref, gate_ref, og_ref, rw_ref, ready_ref, out_ref, tie_ref):
    del ready_ref
    me = me_ref[0]
    mine = s_ref[pl.ds(me // 16, PEERS, stride=4), :]
    offset = ((me // 4) % 4) * 32 + (me % 4) * CAP
    mine = pltpu.roll(mine, (128 - offset) % 128, axis=1)
    code = code_ref[...]
    sdg = jnp.zeros((PEERS, TOK), F32)
    for c in range(CAP):
        sdg = jnp.where(code == c, mine[:, c : c + 1], sdg)
    total = jnp.sum(sdg, axis=0, keepdims=True)
    logit_grad = (sdg - gate_ref[...] * total).astype(BF16)
    part = dot(logit_grad, rw_ref[...], 0, 0)
    out_ref[...] = (og_ref[...].astype(F32) + part).astype(BF16)
    tie_ref[...] = total[:, :1] + jnp.zeros((8, 128), F32)


def router_kernel(s_ref, code_ref, gate_ref, cols_ref, spread_ref, tie_ref, out_ref, lg_ref):
    del tie_ref
    lane = iota((PEERS, 128), 1)
    for t in range(4):
        tile = s_ref[pl.ds(t, PEERS, stride=4), :]
        for q in range(4):
            g = t * 4 + q
            x = pltpu.roll(tile, 128 - 32 * q, axis=1) if q else tile
            x = jnp.where(lane < 24, x, 0.0)
            hi = x.astype(BF16).astype(F32)
            rest = x - hi
            mid = rest.astype(BF16).astype(F32)
            low = (rest - mid).astype(BF16).astype(F32)
            z = hi + pltpu.roll(mid, 32, axis=1) + pltpu.roll(low, 64, axis=1)
            wide = dot(z.astype(BF16), spread_ref[...], 1, 0)
            code = code_ref[g]
            sdg = jnp.zeros((PEERS, 128), F32)
            for c in range(CAP):
                sdg = jnp.where(code == c, wide[:, c * 128 : (c + 1) * 128], sdg)
            total = jnp.sum(sdg, axis=0, keepdims=True)
            lg_ref[:, g * 128 : (g + 1) * 128] = (sdg - gate_ref[g] * total).astype(BF16)
    out_ref[...] = dot(cols_ref[...].astype(BF16), lg_ref[...], 1, 1)


def call(kernel, outs, scratch=(), flops=0, moved=0, **kw):
    return pl.pallas_call(
        kernel,
        out_shape=outs,
        scratch_shapes=list(scratch),
        compiler_params=pltpu.CompilerParams(vmem_limit_bytes=32 << 20),
        cost_estimate=pl.CostEstimate(flops=flops, bytes_accessed=moved, transcendentals=0),
        **kw,
    )


def whole():
    return pl.BlockSpec(memory_space=pltpu.VMEM)


def struct(shape, dtype):
    return jax.ShapeDtypeStruct(shape, dtype)


def pack(og, li, rw, ids):
    return call(
        pack_kernel,
        (
            struct((PEERS, CHUNK, WIDE), BF16),
            struct((PEERS, TOK), F32),
            struct((PEERS, TOK), F32),
        ),
        [pltpu.VMEM((PEERS, WIDE), F32), pltpu.VMEM((PEERS, WIDE), F32)],
        flops=10**9,
        moved=2 * 10**6,
        name="pack",
    )(og, li, rw, ids)


def expert(recv, w, h, perm):
    return call(
        expert_kernel,
        (struct((SLOTS, SLOTS), BF16), struct((PEERS * 4, 128), F32)),
        [pltpu.VMEM((SLOTS, PARTS * WIDE), BF16)],
        flops=12 * 10**8,
        moved=4 * 10**6,
        grid=(1,),
        in_specs=[
            pl.BlockSpec((PEERS, ROWS, WIDE), lambda i: (0, 0, 0)),
            pl.BlockSpec(w.shape, lambda i: (0, 0)),
            pl.BlockSpec(h.shape, lambda i: (0, 0)),
            pl.BlockSpec(perm.shape, lambda i: (0, 0)),
        ],
        out_specs=(
            pl.BlockSpec((SLOTS, SLOTS), lambda i: (0, 0)),
            pl.BlockSpec((PEERS * 4, 128), lambda i: (0, 0)),
        ),
        name="expert",
    )(recv, w, h, perm)


def side(recv, sdg):
    return call(
        side_kernel,
        (
            struct((GROUPS, PEERS, 128), F32),
            struct((GROUPS, PEERS, 128), F32),
            struct((TOK, PEERS * TOK), F32),
            struct((8, 128), F32),
        ),
        flops=10**8,
        moved=2 * 10**6,
        grid=(1,),
        in_specs=[
            pl.BlockSpec((PEERS, 8, WIDE), lambda i: (0, ROWS // 8, 0)),
            pl.BlockSpec((8, 128), lambda i: (0, 0)),
        ],
        out_specs=(
            pl.BlockSpec((GROUPS, PEERS, 128), lambda i: (0, 0, 0)),
            pl.BlockSpec((GROUPS, PEERS, 128), lambda i: (0, 0, 0)),
            pl.BlockSpec((TOK, PEERS * TOK), lambda i: (0, 0)),
            pl.BlockSpec((8, 128), lambda i: (0, 0)),
        ),
        name="side",
    )(recv, sdg)


def input_grads(me, s, code, gate, og, rw, ready):
    return call(
        input_kernel,
        (struct(og.shape, BF16), struct((8, 128), F32)),
        flops=10**7,
        moved=10**6,
        in_specs=[pl.BlockSpec(memory_space=pltpu.SMEM)] + [whole()] * 6,
        name="inputs",
    )(me, s, code, gate, og, rw, ready)


def router_grads(s, code, gate, cols, spread, tie):
    return call(
        router_kernel,
        struct((TOK, PEERS), F32),
        [pltpu.VMEM((PEERS, PEERS * TOK), BF16)],
        flops=3 * 10**8,
        moved=2 * 10**6,
        name="router",
    )(s, code, gate, cols, spread, tie)


def exchange(x):
    return lax.all_to_all(x, "expert", split_axis=0, concat_axis=0, tiled=True)


def shards(out_grad, layer_input, router_weight, expert_ids, hidden_act, down_weight):
    og, li = out_grad[0], layer_input[0]
    rw = jnp.swapaxes(router_weight[0], 0, 1)
    ids = jnp.swapaxes(expert_ids[0], 0, 1)
    me = lax.axis_index("expert").astype(jnp.int32).reshape(1)
    send, gate, code = pack(og, li, rw, ids)
    recv = exchange(send)
    hidden_grad, sdg = expert(
        recv, down_weight[0, 0], hidden_act[0, 0], jnp.asarray(compaction(), BF16)
    )
    back = exchange(sdg.reshape(PEERS, 4, 128)).reshape(PEERS * 4, 128)
    all_gate, all_code, cols, ready = side(recv, sdg)
    input_grad, tie = input_grads(me, back, code, gate, og, rw, ready)
    sections = lax.axis_size("section")
    sent = lax.ppermute(
        input_grad[None], "section", [(i, (i - 1) % sections) for i in range(sections)]
    )
    router_grad = router_grads(
        back, all_code, all_gate, cols, jnp.asarray(spreading(), BF16), tie
    )
    return sent, hidden_grad[None, None], router_grad[None]


def solution(mesh):
    placed = (
        P("section", "expert", None),
        P("section", "expert", None),
        P("section", None, None),
        P("section", "expert", None),
        P("section", "expert", None, None),
        P("section", "expert", None, None),
    )
    return jax.shard_map(
        shards,
        mesh=mesh,
        in_specs=placed,
        out_specs=(
            P("section", "expert", None),
            P("section", "expert", None, None),
            P("section", "expert", None),
        ),
        check_vma=False,
    )
```

```python
import jax
import jax.numpy as jnp
import numpy as np
from jax import lax
from jax.experimental import pallas as pl
from jax.experimental.pallas import tpu as pltpu
from jax.sharding import PartitionSpec as P

F32 = jnp.float32
BF16 = jnp.bfloat16
PEERS = 64
CAP = 6
TOK = 32
WIDE = 256
PARTS = 8
ROWS = PARTS * CAP
CHUNK = ROWS + 8
SLOTS = PEERS * CAP
GROUPS = 16


def dot(a, b, ca, cb):
    return lax.dot_general(a, b, (((ca,), (cb,)), ((), ())), preferred_element_type=F32)


def iota(shape, dim):
    return lax.broadcasted_iota(jnp.int32, shape, dim)


def compaction():
    p = np.zeros((8 * ROWS, 8 * ROWS), np.float32)
    for part in range(PARTS):
        for b in range(8):
            for c in range(CAP):
                p[part * ROWS + b * CAP + c, b * ROWS + part * CAP + c] = 1
    return p


def spreading():
    row, lane = iota((128, CAP * 128), 0), iota((128, CAP * 128), 1)
    slot = ((lane // TOK) & 3) * CAP + lane // 128
    return jnp.where(((row & 31) == slot) & (row < 96), 1.0, 0.0).astype(BF16)


def pack_kernel(
    og_hbm, li_hbm, rw_hbm, ids_hbm, send_ref, gate_ref, code_ref,
    og_ref, li_ref, rw_ref, ids_ref, gt_ref, ct_ref, sems,
):
    pairs = ((ids_hbm, ids_ref), (rw_hbm, rw_ref), (li_hbm, li_ref), (og_hbm, og_ref))
    copies = [pltpu.make_async_copy(a, b, sems.at[i]) for i, (a, b) in enumerate(pairs)]
    for copy in copies:
        copy.start()
    copies[0].wait()
    ids = ids_ref[...]
    copies[1].wait()
    copies[2].wait()
    logits = dot(rw_ref[...], li_ref[...], 1, 1)
    expert = iota((PEERS, TOK), 0)
    named = jnp.zeros((PEERS, TOK), F32)
    for k in range(8):
        named = jnp.where(ids[k : k + 1, :] == expert, 1.0, named)
    weights = jnp.where(named > 0.5, jnp.exp(logits), 0.0)
    gates = (weights / jnp.sum(weights, axis=0, keepdims=True)).astype(BF16)
    token = iota((TOK, WIDE), 0)
    lane = iota((TOK, WIDE), 1) & (TOK - 1)
    tile = jnp.where(token == lane, 1.0, 0.0).astype(BF16)
    ahead = jnp.where(token < lane, 1.0, 0.0).astype(BF16)
    named_b = named.astype(BF16)
    code = jnp.where(dot(named_b, tile, 1, 0) > 0.5, dot(named_b, ahead, 1, 0), -1.0)
    ct_ref[...] = code
    gt_ref[...] = dot(gates, tile, 1, 0)
    gates_f = gates.astype(F32)
    gate_ref[...] = gates_f
    code_ref[...] = code[:, :TOK]

    choice = iota((8, TOK), 0)
    compact = jnp.zeros((8, TOK), F32)
    for k in range(8):
        one = jnp.sum(jnp.where(ids[k : k + 1, :] == expert, gates_f, 0.0), axis=0, keepdims=True)
        compact = jnp.where(choice == k, one, compact)
    t128, l128 = iota((TOK, 128), 0), iota((TOK, 128), 1)
    put_ids = jnp.where(t128 == l128, 1.0, 0.0).astype(BF16)
    put_gates = jnp.where(t128 + TOK == l128, 1.0, 0.0).astype(BF16)
    info = dot(ids.astype(F32).astype(BF16), put_ids, 1, 0) + dot(
        compact.astype(BF16), put_gates, 1, 0
    )
    send_ref[:, ROWS:, 128:] = jnp.broadcast_to(info.astype(BF16)[None], (PEERS, 8, 128))

    spread = dot(li_ref[...], tile[:, :128], 0, 0).reshape(PEERS, 4, 8, 128)
    quarter = iota((PEERS, 8, 128), 2) // TOK
    columns = spread[:, 0]
    for h in range(1, 4):
        columns = jnp.where(quarter == h, spread[:, h], columns)
    send_ref[:, ROWS:, :128] = columns.astype(BF16)

    copies[3].wait()
    stacked = jnp.concatenate(
        [og_ref[:, j * WIDE : (j + 1) * WIDE] for j in range(PARTS)], axis=0
    )
    row = iota((ROWS, WIDE), 0)
    part = jnp.zeros((ROWS, WIDE), jnp.int32)
    for j in range(1, PARTS):
        part = part + jnp.where(row >= j * CAP, 1, 0)
    slot = jnp.where(iota((ROWS, WIDE), 1) // TOK == part, row - part * CAP, -2).astype(F32)

    def step(i, carry):
        picks = []
        for u in range(8):
            at = pl.ds(i * 8 + u, 1)
            hit = jnp.broadcast_to(ct_ref[at, :], (ROWS, WIDE)) == slot
            picks.append(
                jnp.where(hit, jnp.broadcast_to(gt_ref[at, :], (ROWS, WIDE)), 0.0).astype(BF16)
            )
        rows = dot(jnp.concatenate(picks, axis=0), stacked, 1, 0).astype(BF16)
        send_ref[pl.ds(i * 8, 8), :ROWS, :] = rows.reshape(8, ROWS, WIDE)
        return carry

    lax.fori_loop(0, PEERS // 8, step, 0)


def expert_kernel(recv_ref, w_ref, h_ref, perm_ref, hg_ref, sdg_ref, rows_ref):
    perm = perm_ref[...]
    for g in range(8):
        chunk = recv_ref[g * 8 : (g + 1) * 8, :, :].reshape(8 * ROWS, WIDE)
        moved = dot(perm, chunk, 1, 0).astype(BF16)
        for j in range(PARTS):
            rows_ref[g * ROWS : (g + 1) * ROWS, j * WIDE : (j + 1) * WIDE] = moved[
                j * ROWS : (j + 1) * ROWS
            ]
    grad = dot(rows_ref[...], w_ref[...], 1, 1)
    hg_ref[...] = grad.astype(BF16)
    prod = grad * h_ref[...].astype(F32)
    part = prod[:, :128] + prod[:, 128:256] + prod[:, 256:]
    gap = jnp.zeros((8, 128), F32)
    pieces = []
    for g in range(GROUPS):
        pieces += [part[g * 24 : (g + 1) * 24], gap]
    padded = jnp.concatenate(pieces, axis=0)
    line = jnp.sum(padded.T, axis=0, keepdims=True)
    which = iota((8, 128), 0) & 3
    out = jnp.zeros((8, 128), F32)
    for t in range(4):
        out = jnp.where(which == t, line[:, t * 128 : (t + 1) * 128], out)
    sdg_ref[...] = jnp.broadcast_to(out[None], (PEERS // 2, 8, 128)).reshape(PEERS * 4, 128)


def side_kernel(ext_ref, sdg_ref, gate_ref, code_ref, cols_ref, ready_ref):
    ready_ref[...] = sdg_ref[...]
    expert = iota((PEERS, 128), 0).astype(F32)
    row, col = iota((128, 128), 0), iota((128, 128), 1)
    ahead = jnp.where((row // TOK == col // TOK) & (row < col), 1.0, 0.0).astype(BF16)
    quarter = iota((8, 128), 1) // TOK

    def gather(blocks, at):
        out = None
        for i, block in enumerate(blocks):
            shift = (i - at) * TOK % 128
            moved = pltpu.roll(block, shift, axis=1) if shift else block
            out = moved if out is None else jnp.where(quarter == i, moved, out)
        return out

    for g in range(GROUPS):
        info = [ext_ref[4 * g + i, :, 128:].astype(F32) for i in range(4)]
        ids, gates = gather(info, 0), gather(info, 1)
        named = jnp.zeros((PEERS, 128), F32)
        dense = jnp.zeros((PEERS, 128), F32)
        for k in range(8):
            hit = ids[k : k + 1, :] == expert
            named = jnp.where(hit, 1.0, named)
            dense = jnp.where(hit, gates[k : k + 1, :], dense)
        rank = dot(named.astype(BF16), ahead, 1, 0)
        code_ref[g] = jnp.where(named > 0.5, rank, -1.0)
        gate_ref[g] = dense
        cols = [ext_ref[4 * g + i, :, :128].astype(F32) for i in range(4)]
        for h in range(4):
            cols_ref[h * 8 : (h + 1) * 8, g * 128 : (g + 1) * 128] = gather(cols, h)


def input_kernel(
    me_ref, s_ref, code_ref, gate_ref, ready_ref, og_hbm, rw_hbm, out_ref, tie_ref, og_ref, rw_ref, sems
):
    del ready_ref
    copies = [
        pltpu.make_async_copy(rw_hbm, rw_ref, sems.at[0]),
        pltpu.make_async_copy(og_hbm, og_ref, sems.at[1]),
    ]
    for copy in copies:
        copy.start()
    me = me_ref[0]
    mine = s_ref[pl.ds(me // 16, PEERS, stride=4), :]
    offset = ((me // 4) % 4) * 32 + (me % 4) * CAP
    mine = pltpu.roll(mine, (128 - offset) % 128, axis=1)
    code = code_ref[...]
    sdg = jnp.zeros((PEERS, TOK), F32)
    for c in range(CAP):
        sdg = jnp.where(code == c, mine[:, c : c + 1], sdg)
    total = jnp.sum(sdg, axis=0, keepdims=True)
    logit_grad = (sdg - gate_ref[...] * total).astype(BF16)
    for copy in copies:
        copy.wait()
    part = dot(logit_grad, rw_ref[...], 0, 0)
    out_ref[...] = (og_ref[...].astype(F32) + part).astype(BF16)
    tie_ref[...] = total[:, :1] + jnp.zeros((8, 128), F32)


def router_kernel(s_ref, code_ref, gate_ref, cols_ref, tie_ref, out_ref, spread_ref, lg_ref):
    del tie_ref
    spread_ref[...] = spreading()
    lane = iota((PEERS, 128), 1)
    for t in range(4):
        tile = s_ref[pl.ds(t, PEERS, stride=4), :]
        for q in range(4):
            g = t * 4 + q
            x = pltpu.roll(tile, 128 - 32 * q, axis=1) if q else tile
            x = jnp.where(lane < 24, x, 0.0)
            hi = x.astype(BF16).astype(F32)
            rest = x - hi
            mid = rest.astype(BF16).astype(F32)
            low = (rest - mid).astype(BF16).astype(F32)
            z = hi + pltpu.roll(mid, 32, axis=1) + pltpu.roll(low, 64, axis=1)
            wide = dot(z.astype(BF16), spread_ref[...], 1, 0)
            code = code_ref[g]
            sdg = jnp.zeros((PEERS, 128), F32)
            for c in range(CAP):
                sdg = jnp.where(code == c, wide[:, c * 128 : (c + 1) * 128], sdg)
            total = jnp.sum(sdg, axis=0, keepdims=True)
            lg_ref[:, g * 128 : (g + 1) * 128] = (sdg - gate_ref[g] * total).astype(BF16)
    out_ref[...] = dot(cols_ref[...].astype(BF16), lg_ref[...], 1, 1)


def call(kernel, outs, scratch=(), flops=0, moved=0, **kw):
    return pl.pallas_call(
        kernel,
        out_shape=outs,
        scratch_shapes=list(scratch),
        compiler_params=pltpu.CompilerParams(vmem_limit_bytes=kw.pop("limit", 32) << 20),
        cost_estimate=pl.CostEstimate(flops=flops, bytes_accessed=moved, transcendentals=0),
        **kw,
    )


def whole():
    return pl.BlockSpec(memory_space=pltpu.VMEM)


def far():
    return pl.BlockSpec(memory_space=pltpu.HBM)


def struct(shape, dtype):
    return jax.ShapeDtypeStruct(shape, dtype)


def pack(og, li, rw, ids):
    return call(
        pack_kernel,
        (
            struct((PEERS, CHUNK, WIDE), BF16),
            struct((PEERS, TOK), F32),
            struct((PEERS, TOK), F32),
        ),
        [pltpu.VMEM(a.shape, a.dtype) for a in (og, li, rw, ids)]
        + [pltpu.VMEM((PEERS, WIDE), F32)] * 2
        + [pltpu.SemaphoreType.DMA((4,))],
        flops=10**9,
        moved=2 * 10**6,
        in_specs=[far()] * 4,
        name="pack",
    )(og, li, rw, ids)


def expert(recv, w, h, perm):
    return call(
        expert_kernel,
        (struct((SLOTS, SLOTS), BF16), struct((PEERS * 4, 128), F32)),
        [pltpu.VMEM((SLOTS, PARTS * WIDE), BF16)],
        flops=12 * 10**8,
        moved=4 * 10**6,
        grid=(1,),
        in_specs=[
            pl.BlockSpec((PEERS, ROWS, WIDE), lambda i: (0, 0, 0)),
            pl.BlockSpec(w.shape, lambda i: (0, 0)),
            pl.BlockSpec(h.shape, lambda i: (0, 0)),
            pl.BlockSpec(perm.shape, lambda i: (0, 0)),
        ],
        out_specs=(
            pl.BlockSpec((SLOTS, SLOTS), lambda i: (0, 0)),
            pl.BlockSpec((PEERS * 4, 128), lambda i: (0, 0)),
        ),
        name="expert",
    )(recv, w, h, perm)


def side(recv, sdg):
    outs = (
        struct((GROUPS, PEERS, 128), F32),
        struct((GROUPS, PEERS, 128), F32),
        struct((TOK, PEERS * TOK), F32),
        struct((8, 128), F32),
    )
    return call(
        side_kernel,
        outs,
        flops=10**8,
        moved=2 * 10**6,
        grid=(1,),
        in_specs=[
            pl.BlockSpec((PEERS, 8, WIDE), lambda i: (0, ROWS // 8, 0)),
            pl.BlockSpec((8, 128), lambda i: (0, 0)),
        ],
        out_specs=tuple(whole() for _ in outs),
        name="side",
    )(recv, sdg)


def input_grads(me, s, code, gate, ready, og, rw):
    return call(
        input_kernel,
        (struct(og.shape, BF16), struct((8, 128), F32)),
        [pltpu.VMEM(a.shape, a.dtype) for a in (og, rw)] + [pltpu.SemaphoreType.DMA((2,))],
        flops=10**7,
        moved=10**6,
        in_specs=[pl.BlockSpec(memory_space=pltpu.SMEM)] + [whole()] * 4 + [far()] * 2,
        name="inputs",
    )(me, s, code, gate, ready, og, rw)


def router_grads(s, code, gate, cols, tie):
    return call(
        router_kernel,
        struct((TOK, PEERS), F32),
        [pltpu.VMEM((128, CAP * 128), BF16), pltpu.VMEM((PEERS, PEERS * TOK), BF16)],
        flops=3 * 10**8,
        moved=2 * 10**6,
        name="router",
    )(s, code, gate, cols, tie)


def exchange(x):
    return lax.all_to_all(x, "expert", split_axis=0, concat_axis=0, tiled=True)


def shards(out_grad, layer_input, router_weight, expert_ids, hidden_act, down_weight):
    og, li = out_grad[0], layer_input[0]
    rw = jnp.swapaxes(router_weight[0], 0, 1)
    ids = jnp.swapaxes(expert_ids[0], 0, 1)
    og, li, rw, ids = [
        pltpu.with_memory_space_constraint(a, pltpu.HBM) for a in (og, li, rw, ids)
    ]
    me = lax.axis_index("expert").astype(jnp.int32).reshape(1)
    send, gate, code = pack(og, li, rw, ids)
    recv = exchange(send)
    hidden_grad, sdg = expert(
        recv, down_weight[0, 0], hidden_act[0, 0], jnp.asarray(compaction(), BF16)
    )
    back = exchange(sdg.reshape(PEERS, 4, 128)).reshape(PEERS * 4, 128)
    all_gate, all_code, cols, ready = side(recv, sdg)
    input_grad, tie = input_grads(me, back, code, gate, ready, og, rw)
    sections = lax.axis_size("section")
    sent = lax.ppermute(
        input_grad[None], "section", [(i, (i - 1) % sections) for i in range(sections)]
    )
    router_grad = router_grads(back, all_code, all_gate, cols, tie)
    return sent, hidden_grad[None, None], router_grad[None]


def solution(mesh):
    placed = (
        P("section", "expert", None),
        P("section", "expert", None),
        P("section", None, None),
        P("section", "expert", None),
        P("section", "expert", None, None),
        P("section", "expert", None, None),
    )
    return jax.shard_map(
        shards,
        mesh=mesh,
        in_specs=placed,
        out_specs=(
            P("section", "expert", None),
            P("section", "expert", None, None),
            P("section", "expert", None),
        ),
        check_vma=False,
    )
```

```python
import jax
import jax.numpy as jnp
import numpy as np
from jax import lax
from jax.experimental import pallas as pl
from jax.experimental.pallas import tpu as pltpu
from jax.sharding import PartitionSpec as P

F32 = jnp.float32
BF16 = jnp.bfloat16
PEERS = 64
CAP = 6
TOK = 32
WIDE = 256
PARTS = 8
ROWS = PARTS * CAP
CHUNK = ROWS + 8
SLOTS = PEERS * CAP
GROUPS = 16


def dot(a, b, ca, cb):
    return lax.dot_general(a, b, (((ca,), (cb,)), ((), ())), preferred_element_type=F32)


def iota(shape, dim):
    return lax.broadcasted_iota(jnp.int32, shape, dim)


def compaction():
    p = np.zeros((4 * ROWS, 4 * ROWS), np.float32)
    for part in range(PARTS):
        for b in range(4):
            for c in range(CAP):
                p[part * 4 * CAP + b * CAP + c, b * ROWS + part * CAP + c] = 1
    return p


def spreading():
    row, lane = iota((128, CAP * 128), 0), iota((128, CAP * 128), 1)
    slot = ((lane // TOK) & 3) * CAP + lane // 128
    return jnp.where(((row & 31) == slot) & (row < 96), 1.0, 0.0).astype(BF16)


def pack_kernel(
    og_hbm, li_hbm, rw_hbm, ids_hbm, send_ref,
    og_ref, li_ref, rw_ref, ids_ref, gt_ref, ct_ref, sems,
):
    pairs = ((ids_hbm, ids_ref), (rw_hbm, rw_ref), (li_hbm, li_ref), (og_hbm, og_ref))
    copies = [pltpu.make_async_copy(a, b, sems.at[i]) for i, (a, b) in enumerate(pairs)]
    for copy in copies:
        copy.start()
    copies[0].wait()
    ids = ids_ref[...]
    expert = iota((PEERS, TOK), 0)
    named = jnp.zeros((PEERS, TOK), F32)
    for k in range(8):
        named = jnp.where(ids[k : k + 1, :] == expert, 1.0, named)
    token = iota((TOK, WIDE), 0)
    lane = iota((TOK, WIDE), 1) & (TOK - 1)
    tile = jnp.where(token == lane, 1.0, 0.0).astype(BF16)
    ahead = jnp.where(token < lane, 1.0, 0.0).astype(BF16)
    named_b = named.astype(BF16)
    code = jnp.where(dot(named_b, tile, 1, 0) > 0.5, dot(named_b, ahead, 1, 0), -1.0)
    ct_ref[...] = code
    copies[1].wait()
    copies[2].wait()
    logits = dot(rw_ref[...], li_ref[...], 1, 1)
    weights = jnp.where(named > 0.5, jnp.exp(logits), 0.0)
    gates = (weights / jnp.sum(weights, axis=0, keepdims=True)).astype(BF16)
    gt_ref[...] = dot(gates, tile, 1, 0)
    gates_f = gates.astype(F32)

    choice = iota((8, TOK), 0)
    compact = jnp.zeros((8, TOK), F32)
    for k in range(8):
        one = jnp.sum(jnp.where(ids[k : k + 1, :] == expert, gates_f, 0.0), axis=0, keepdims=True)
        compact = jnp.where(choice == k, one, compact)
    t128, l128 = iota((TOK, 128), 0), iota((TOK, 128), 1)
    put_ids = jnp.where(t128 == l128, 1.0, 0.0).astype(BF16)
    put_gates = jnp.where(t128 + TOK == l128, 1.0, 0.0).astype(BF16)
    info = dot(ids.astype(F32).astype(BF16), put_ids, 1, 0) + dot(
        compact.astype(BF16), put_gates, 1, 0
    )
    send_ref[:, ROWS:, 128:] = jnp.broadcast_to(info.astype(BF16)[None], (PEERS, 8, 128))

    spread = dot(li_ref[...], tile[:, :128], 0, 0).reshape(PEERS, 4, 8, 128)
    quarter = iota((PEERS, 8, 128), 2) // TOK
    columns = spread[:, 0]
    for h in range(1, 4):
        columns = jnp.where(quarter == h, spread[:, h], columns)
    send_ref[:, ROWS:, :128] = columns.astype(BF16)

    copies[3].wait()
    stacked = jnp.concatenate(
        [og_ref[:, j * WIDE : (j + 1) * WIDE] for j in range(PARTS)], axis=0
    )
    row = iota((ROWS, WIDE), 0)
    part = jnp.zeros((ROWS, WIDE), jnp.int32)
    for j in range(1, PARTS):
        part = part + jnp.where(row >= j * CAP, 1, 0)
    slot = jnp.where(iota((ROWS, WIDE), 1) // TOK == part, row - part * CAP, -2).astype(F32)

    def step(i, carry):
        picks = []
        for u in range(8):
            at = pl.ds(i * 8 + u, 1)
            hit = jnp.broadcast_to(ct_ref[at, :], (ROWS, WIDE)) == slot
            picks.append(
                jnp.where(hit, jnp.broadcast_to(gt_ref[at, :], (ROWS, WIDE)), 0.0).astype(BF16)
            )
        rows = dot(jnp.concatenate(picks, axis=0), stacked, 1, 0).astype(BF16)
        send_ref[pl.ds(i * 8, 8), :ROWS, :] = rows.reshape(8, ROWS, WIDE)
        return carry

    lax.fori_loop(0, PEERS // 8, step, 0)


def expert_kernel(recv_ref, w_ref, h_ref, perm_ref, hg_ref, sdg_ref, rows_ref):
    perm = perm_ref[...]
    for g in range(8):
        halves = []
        for h in range(2):
            b = g * 8 + h * 4
            chunk = recv_ref[b : b + 4, :ROWS, :].reshape(4 * ROWS, WIDE)
            halves.append(dot(perm, chunk, 1, 0))
        for j in range(PARTS):
            piece = jnp.concatenate([m[j * 24 : (j + 1) * 24] for m in halves], axis=0)
            rows_ref[g * ROWS : (g + 1) * ROWS, j * WIDE : (j + 1) * WIDE] = piece.astype(BF16)
    grad = dot(rows_ref[...], w_ref[...], 1, 1)
    hg_ref[...] = grad.astype(BF16)
    prod = grad * h_ref[...].astype(F32)
    part = prod[:, :128] + prod[:, 128:256] + prod[:, 256:]
    gap = jnp.zeros((8, 128), F32)
    pieces = []
    for g in range(GROUPS):
        pieces += [part[g * 24 : (g + 1) * 24], gap]
    padded = jnp.concatenate(pieces, axis=0)
    line = jnp.sum(padded.T, axis=0, keepdims=True)
    which = iota((8, 128), 0) & 3
    out = jnp.zeros((8, 128), F32)
    for t in range(4):
        out = jnp.where(which == t, line[:, t * 128 : (t + 1) * 128], out)
    sdg_ref[...] = jnp.broadcast_to(out[None], (PEERS // 2, 8, 128)).reshape(PEERS * 4, 128)


def side_kernel(recv_ref, sdg_ref, gate_ref, code_ref, cols_ref, ready_ref):
    ready_ref[...] = sdg_ref[:8, :]
    expert = iota((PEERS, 128), 0).astype(F32)
    row, col = iota((128, 128), 0), iota((128, 128), 1)
    ahead = jnp.where((row // TOK == col // TOK) & (row < col), 1.0, 0.0).astype(BF16)
    quarter = iota((8, 128), 1) // TOK

    def gather(blocks, at):
        out = None
        for i, block in enumerate(blocks):
            shift = (i - at) * TOK % 128
            moved = pltpu.roll(block, shift, axis=1) if shift else block
            out = moved if out is None else jnp.where(quarter == i, moved, out)
        return out

    for g in range(GROUPS):
        info = [recv_ref[4 * g + i, ROWS:, 128:].astype(F32) for i in range(4)]
        ids, gates = gather(info, 0), gather(info, 1)
        named = jnp.zeros((PEERS, 128), F32)
        dense = jnp.zeros((PEERS, 128), F32)
        for k in range(8):
            hit = ids[k : k + 1, :] == expert
            named = jnp.where(hit, 1.0, named)
            dense = jnp.where(hit, gates[k : k + 1, :], dense)
        rank = dot(named.astype(BF16), ahead, 1, 0)
        code_ref[g] = jnp.where(named > 0.5, rank, -1.0)
        gate_ref[g] = dense
        cols = [recv_ref[4 * g + i, ROWS:, :128].astype(F32) for i in range(4)]
        for h in range(4):
            cols_ref[h * 8 : (h + 1) * 8, g * 128 : (g + 1) * 128] = gather(cols, h)


def logit_kernel(me_ref, s_ref, code_ref, gate_ref, out_ref):
    me = me_ref[0]
    mine = s_ref[pl.ds(me // 16, PEERS, stride=4), :]
    offset = ((me // 4) % 4) * 32 + (me % 4) * CAP
    mine = pltpu.roll(mine, (128 - offset) % 128, axis=1)
    back = (128 - (me % 4) * TOK) % 128
    code = pltpu.roll(code_ref[me // 4], back, axis=1)[:, :TOK]
    gate = pltpu.roll(gate_ref[me // 4], back, axis=1)[:, :TOK]
    sdg = jnp.zeros((PEERS, TOK), F32)
    for c in range(CAP):
        sdg = jnp.where(code == c, mine[:, c : c + 1], sdg)
    total = jnp.sum(sdg, axis=0, keepdims=True)
    out_ref[...] = (sdg - gate * total).astype(BF16)


def input_kernel(lg_ref, og_ref, rw_ref, out_ref):
    part = dot(lg_ref[...], rw_ref[...], 0, 0)
    out_ref[...] = (og_ref[...].astype(F32) + part).astype(BF16)


def router_kernel(s_ref, code_ref, gate_ref, cols_ref, tie_ref, out_ref, spread_ref, lg_ref):
    del tie_ref
    spread_ref[...] = spreading()
    lane = iota((PEERS, 128), 1)
    for t in range(4):
        tile = s_ref[pl.ds(t, PEERS, stride=4), :]
        for q in range(4):
            g = t * 4 + q
            x = pltpu.roll(tile, 128 - 32 * q, axis=1) if q else tile
            x = jnp.where(lane < 24, x, 0.0)
            hi = x.astype(BF16).astype(F32)
            rest = x - hi
            mid = rest.astype(BF16).astype(F32)
            low = (rest - mid).astype(BF16).astype(F32)
            z = hi + pltpu.roll(mid, 32, axis=1) + pltpu.roll(low, 64, axis=1)
            wide = dot(z.astype(BF16), spread_ref[...], 1, 0)
            code = code_ref[g]
            sdg = jnp.zeros((PEERS, 128), F32)
            for c in range(CAP):
                sdg = jnp.where(code == c, wide[:, c * 128 : (c + 1) * 128], sdg)
            total = jnp.sum(sdg, axis=0, keepdims=True)
            lg_ref[:, g * 128 : (g + 1) * 128] = (sdg - gate_ref[g] * total).astype(BF16)
    out_ref[...] = dot(cols_ref[...].astype(BF16), lg_ref[...], 1, 1)


def call(kernel, outs, scratch=(), flops=0, moved=0, **kw):
    return pl.pallas_call(
        kernel,
        out_shape=outs,
        scratch_shapes=list(scratch),
        compiler_params=pltpu.CompilerParams(vmem_limit_bytes=kw.pop("limit", 32) << 20),
        cost_estimate=pl.CostEstimate(flops=flops, bytes_accessed=moved, transcendentals=0),
        **kw,
    )


def whole():
    return pl.BlockSpec(memory_space=pltpu.VMEM)


def far():
    return pl.BlockSpec(memory_space=pltpu.HBM)


def struct(shape, dtype):
    return jax.ShapeDtypeStruct(shape, dtype)


def pack(og, li, rw, ids):
    return call(
        pack_kernel,
        struct((PEERS, CHUNK, WIDE), BF16),
        [pltpu.VMEM(a.shape, a.dtype) for a in (og, li, rw, ids)]
        + [pltpu.VMEM((PEERS, WIDE), F32)] * 2
        + [pltpu.SemaphoreType.DMA((4,))],
        flops=10**9,
        moved=2 * 10**6,
        in_specs=[far()] * 4,
        name="pack",
    )(og, li, rw, ids)


def expert(recv, w, h, perm):
    return call(
        expert_kernel,
        (struct((SLOTS, SLOTS), BF16), struct((PEERS * 4, 128), F32)),
        [pltpu.VMEM((SLOTS, PARTS * WIDE), BF16)],
        flops=12 * 10**8,
        moved=4 * 10**6,
        name="expert",
    )(recv, w, h, perm)


def side(recv, sdg):
    outs = (
        struct((GROUPS, PEERS, 128), F32),
        struct((GROUPS, PEERS, 128), F32),
        struct((TOK, PEERS * TOK), F32),
        struct((8, 128), F32),
    )
    return call(
        side_kernel,
        outs,
        flops=10**8,
        moved=2 * 10**6,
        name="side",
    )(recv, sdg)


def logit_grads(me, s, code, gate):
    return call(
        logit_kernel,
        struct((PEERS, TOK), BF16),
        flops=10**6,
        moved=2 * 10**5,
        in_specs=[pl.BlockSpec(memory_space=pltpu.SMEM)] + [whole()] * 3,
        name="logits",
    )(me, s, code, gate)


def input_grads(lg, og, rw):
    return call(
        input_kernel,
        struct(og.shape, BF16),
        flops=10**7,
        moved=10**6,
        name="inputs",
    )(lg, og, rw)


def router_grads(s, code, gate, cols, tie):
    return call(
        router_kernel,
        struct((TOK, PEERS), F32),
        [pltpu.VMEM((128, CAP * 128), BF16), pltpu.VMEM((PEERS, PEERS * TOK), BF16)],
        flops=3 * 10**8,
        moved=2 * 10**6,
        name="router",
    )(s, code, gate, cols, tie)


def shifted(x):
    n = lax.axis_size("section")
    return lax.ppermute(x, "section", [(i, (i - 1) % n) for i in range(n)])


def exchange(x):
    return lax.all_to_all(x, "expert", split_axis=0, concat_axis=0, tiled=True)


def shards(out_grad, layer_input, router_weight, expert_ids, hidden_act, down_weight):
    og, li = out_grad[0], layer_input[0]
    rw = jnp.swapaxes(router_weight[0], 0, 1)
    ids = jnp.swapaxes(expert_ids[0], 0, 1)
    far_args = [pltpu.with_memory_space_constraint(a, pltpu.HBM) for a in (og, li, rw, ids)]
    me = lax.axis_index("expert").astype(jnp.int32).reshape(1)
    send = pack(*far_args)
    recv = exchange(send)
    hidden_grad, sdg = expert(
        recv, down_weight[0, 0], hidden_act[0, 0], jnp.asarray(compaction(), BF16)
    )
    back = exchange(sdg.reshape(PEERS, 4, 128)).reshape(PEERS * 4, 128)
    all_gate, all_code, cols, ready = side(recv, sdg)
    og_held, rw_held, _ = lax.optimization_barrier((og, rw, ready))
    og_next, rw_next = shifted(og_held), shifted(rw_held)
    logit_grad = logit_grads(me, back, all_code, all_gate)
    logit_next = shifted(logit_grad)
    router_grad = router_grads(back, all_code, all_gate, cols, logit_grad)
    sent = input_grads(logit_next, og_next, rw_next)[None]
    return sent, hidden_grad[None, None], router_grad[None]


def solution(mesh):
    placed = (
        P("section", "expert", None),
        P("section", "expert", None),
        P("section", None, None),
        P("section", "expert", None),
        P("section", "expert", None, None),
        P("section", "expert", None, None),
    )
    return jax.shard_map(
        shards,
        mesh=mesh,
        in_specs=placed,
        out_specs=(
            P("section", "expert", None),
            P("section", "expert", None, None),
            P("section", "expert", None),
        ),
        check_vma=False,
    )
```

```python
import jax
import jax.numpy as jnp
import numpy as np
from jax import lax
from jax.experimental import pallas as pl
from jax.experimental.pallas import tpu as pltpu
from jax.sharding import PartitionSpec as P

F32 = jnp.float32
BF16 = jnp.bfloat16
PEERS = 64
CAP = 6
TOK = 32
WIDE = 256
PARTS = 8
ROWS = PARTS * CAP
CHUNK = ROWS + 8
SLOTS = PEERS * CAP
GROUPS = 16


def dot(a, b, ca, cb):
    return lax.dot_general(a, b, (((ca,), (cb,)), ((), ())), preferred_element_type=F32)


def iota(shape, dim):
    return lax.broadcasted_iota(jnp.int32, shape, dim)


def compaction():
    p = np.zeros((4 * ROWS, 4 * ROWS), np.float32)
    for part in range(PARTS):
        for b in range(4):
            for c in range(CAP):
                p[part * 4 * CAP + b * CAP + c, b * ROWS + part * CAP + c] = 1
    return p


def spreading():
    row, lane = iota((128, CAP * 128), 0), iota((128, CAP * 128), 1)
    slot = ((lane // TOK) & 3) * CAP + lane // 128
    return jnp.where(((row & 31) == slot) & (row < 96), 1.0, 0.0).astype(BF16)


def pack_kernel(
    og_hbm, li_hbm, rw_hbm, ids_hbm, send_ref, og_ref, li_ref, rw_ref, ids_ref, gt_ref, ct_ref, sems
):
    pairs = ((ids_hbm, ids_ref), (rw_hbm, rw_ref), (li_hbm, li_ref), (og_hbm, og_ref))
    copies = [pltpu.make_async_copy(a, b, sems.at[i]) for i, (a, b) in enumerate(pairs)]
    for copy in copies:
        copy.start()
    copies[0].wait()
    ids = ids_ref[...]
    expert = iota((PEERS, TOK), 0)
    named = jnp.zeros((PEERS, TOK), F32)
    for k in range(8):
        named = jnp.where(ids[k : k + 1, :] == expert, 1.0, named)
    token = iota((TOK, WIDE), 0)
    lane = iota((TOK, WIDE), 1) & (TOK - 1)
    tile = jnp.where(token == lane, 1.0, 0.0).astype(BF16)
    ahead = jnp.where(token < lane, 1.0, 0.0).astype(BF16)
    named_b = named.astype(BF16)
    code = jnp.where(dot(named_b, tile, 1, 0) > 0.5, dot(named_b, ahead, 1, 0), -1.0)
    ct_ref[...] = code
    copies[1].wait()
    copies[2].wait()
    logits = dot(rw_ref[...], li_ref[...], 1, 1)
    weights = jnp.where(named > 0.5, jnp.exp(logits), 0.0)
    gates = (weights / jnp.sum(weights, axis=0, keepdims=True)).astype(BF16)
    gt_ref[...] = dot(gates, tile, 1, 0)
    gates_f = gates.astype(F32)

    choice = iota((8, TOK), 0)
    compact = jnp.zeros((8, TOK), F32)
    for k in range(8):
        one = jnp.sum(jnp.where(ids[k : k + 1, :] == expert, gates_f, 0.0), axis=0, keepdims=True)
        compact = jnp.where(choice == k, one, compact)
    t128, l128 = iota((TOK, 128), 0), iota((TOK, 128), 1)
    put_ids = jnp.where(t128 == l128, 1.0, 0.0).astype(BF16)
    put_gates = jnp.where(t128 + TOK == l128, 1.0, 0.0).astype(BF16)
    info = dot(ids.astype(F32).astype(BF16), put_ids, 1, 0) + dot(
        compact.astype(BF16), put_gates, 1, 0
    )
    send_ref[:, ROWS:, 128:] = jnp.broadcast_to(info.astype(BF16)[None], (PEERS, 8, 128))

    spread = dot(li_ref[...], tile[:, :128], 0, 0).reshape(PEERS, 4, 8, 128)
    quarter = iota((PEERS, 8, 128), 2) // TOK
    columns = spread[:, 0]
    for h in range(1, 4):
        columns = jnp.where(quarter == h, spread[:, h], columns)
    send_ref[:, ROWS:, :128] = columns.astype(BF16)

    copies[3].wait()
    stacked = jnp.concatenate(
        [og_ref[:, j * WIDE : (j + 1) * WIDE] for j in range(PARTS)], axis=0
    )
    row = iota((ROWS, WIDE), 0)
    part = jnp.zeros((ROWS, WIDE), jnp.int32)
    for j in range(1, PARTS):
        part = part + jnp.where(row >= j * CAP, 1, 0)
    slot = jnp.where(iota((ROWS, WIDE), 1) // TOK == part, row - part * CAP, -2).astype(F32)

    def step(i, carry):
        picks = []
        for u in range(8):
            at = pl.ds(i * 8 + u, 1)
            hit = jnp.broadcast_to(ct_ref[at, :], (ROWS, WIDE)) == slot
            picks.append(
                jnp.where(hit, jnp.broadcast_to(gt_ref[at, :], (ROWS, WIDE)), 0.0).astype(BF16)
            )
        rows = dot(jnp.concatenate(picks, axis=0), stacked, 1, 0).astype(BF16)
        send_ref[pl.ds(i * 8, 8), :ROWS, :] = rows.reshape(8, ROWS, WIDE)
        return carry

    lax.fori_loop(0, PEERS // 8, step, 0, unroll=8)


def expert_kernel(recv_ref, w_ref, h_ref, perm_ref, hg_ref, sdg_ref, rows_ref):
    perm = perm_ref[...]
    for g in range(8):
        halves = []
        for h in range(2):
            b = g * 8 + h * 4
            chunk = recv_ref[b : b + 4, :ROWS, :].reshape(4 * ROWS, WIDE)
            halves.append(dot(perm, chunk, 1, 0))
        for j in range(PARTS):
            piece = jnp.concatenate([m[j * 24 : (j + 1) * 24] for m in halves], axis=0)
            rows_ref[g * ROWS : (g + 1) * ROWS, j * WIDE : (j + 1) * WIDE] = piece.astype(BF16)
    grad = dot(rows_ref[...], w_ref[...], 1, 1)
    hg_ref[...] = grad.astype(BF16)
    prod = grad * h_ref[...].astype(F32)
    part = prod[:, :128] + prod[:, 128:256] + prod[:, 256:]
    gap = jnp.zeros((8, 128), F32)
    pieces = []
    for g in range(GROUPS):
        pieces += [part[g * 24 : (g + 1) * 24], gap]
    padded = jnp.concatenate(pieces, axis=0)
    line = jnp.sum(padded.T, axis=0, keepdims=True)
    which = iota((8, 128), 0) & 3
    out = jnp.zeros((8, 128), F32)
    for t in range(4):
        out = jnp.where(which == t, line[:, t * 128 : (t + 1) * 128], out)
    sdg_ref[...] = jnp.broadcast_to(out[None], (PEERS // 2, 8, 128)).reshape(PEERS * 4, 128)


def gather(blocks, at):
    quarter = iota((8, 128), 1) // TOK
    out = None
    for i, block in enumerate(blocks):
        shift = (i - at) * TOK % 128
        moved = pltpu.roll(block, shift, axis=1) if shift else block
        out = moved if out is None else jnp.where(quarter == i, moved, out)
    return out


def side_kernel(recv_ref, hg_ref, gate_ref, code_ref, hg_hbm, sem):
    copy = pltpu.make_async_copy(hg_ref, hg_hbm, sem)
    copy.start()
    expert = iota((PEERS, 128), 0).astype(F32)
    row, col = iota((128, 128), 0), iota((128, 128), 1)
    ahead = jnp.where((row // TOK == col // TOK) & (row < col), 1.0, 0.0).astype(BF16)
    for g in range(GROUPS):
        info = [recv_ref[4 * g + i, ROWS:, 128:].astype(F32) for i in range(4)]
        ids, gates = gather(info, 0), gather(info, 1)
        named = jnp.zeros((PEERS, 128), F32)
        dense = jnp.zeros((PEERS, 128), F32)
        for k in range(8):
            hit = ids[k : k + 1, :] == expert
            named = jnp.where(hit, 1.0, named)
            dense = jnp.where(hit, gates[k : k + 1, :], dense)
        rank = dot(named.astype(BF16), ahead, 1, 0)
        code_ref[g] = jnp.where(named > 0.5, rank, -1.0)
        gate_ref[g] = dense
    copy.wait()


def logit_kernel(me_ref, s_ref, code_ref, gate_ref, out_ref):
    me = me_ref[0]
    mine = s_ref[pl.ds(me // 16, PEERS, stride=4), :]
    offset = ((me // 4) % 4) * 32 + (me % 4) * CAP
    mine = pltpu.roll(mine, (128 - offset) % 128, axis=1)
    back = (128 - (me % 4) * TOK) % 128
    code = pltpu.roll(code_ref[me // 4], back, axis=1)[:, :TOK]
    gate = pltpu.roll(gate_ref[me // 4], back, axis=1)[:, :TOK]
    sdg = jnp.zeros((PEERS, TOK), F32)
    for c in range(CAP):
        sdg = jnp.where(code == c, mine[:, c : c + 1], sdg)
    total = jnp.sum(sdg, axis=0, keepdims=True)
    out_ref[...] = (sdg - gate * total).astype(BF16)


def input_kernel(lg_ref, og_hbm, rw_hbm, out_hbm, og_ref, rw_ref, out_ref, sems):
    spans = [pl.ds(i * 512, 512) for i in range(4)]
    loads = [
        pltpu.make_async_copy(rw_hbm.at[:, at], rw_ref.at[:, at], sems.at[i])
        for i, at in enumerate(spans)
    ] + [pltpu.make_async_copy(og_hbm, og_ref, sems.at[8])]
    stores = [
        pltpu.make_async_copy(out_ref.at[:, at], out_hbm.at[:, at], sems.at[4 + i])
        for i, at in enumerate(spans)
    ]
    for copy in loads:
        copy.start()
    lg = lg_ref[...]
    for i, at in enumerate(spans):
        loads[i].wait()
        part = dot(lg, rw_ref[:, at], 0, 0)
        if i == 0:
            loads[4].wait()
        out_ref[:, at] = (og_ref[:, at].astype(F32) + part).astype(BF16)
        stores[i].start()
    for copy in stores:
        copy.wait()


def router_kernel(
    s_ref, code_ref, gate_ref, recv_ref, tie_ref, out_ref, cols_ref, spread_ref, lg_ref
):
    del tie_ref
    spread_ref[...] = spreading()
    for g in range(GROUPS):
        cols = [recv_ref[4 * g + i, ROWS:, :128].astype(F32) for i in range(4)]
        for h in range(4):
            cols_ref[h * 8 : (h + 1) * 8, g * 128 : (g + 1) * 128] = gather(cols, h)
    lane = iota((PEERS, 128), 1)
    for t in range(4):
        tile = s_ref[pl.ds(t, PEERS, stride=4), :]
        for q in range(4):
            g = t * 4 + q
            x = pltpu.roll(tile, 128 - 32 * q, axis=1) if q else tile
            x = jnp.where(lane < 24, x, 0.0)
            hi = x.astype(BF16).astype(F32)
            rest = x - hi
            mid = rest.astype(BF16).astype(F32)
            low = (rest - mid).astype(BF16).astype(F32)
            z = hi + pltpu.roll(mid, 32, axis=1) + pltpu.roll(low, 64, axis=1)
            wide = dot(z.astype(BF16), spread_ref[...], 1, 0)
            code = code_ref[g]
            sdg = jnp.zeros((PEERS, 128), F32)
            for c in range(CAP):
                sdg = jnp.where(code == c, wide[:, c * 128 : (c + 1) * 128], sdg)
            total = jnp.sum(sdg, axis=0, keepdims=True)
            lg_ref[:, g * 128 : (g + 1) * 128] = (sdg - gate_ref[g] * total).astype(BF16)
    out_ref[...] = dot(cols_ref[...].astype(BF16), lg_ref[...], 1, 1)


def call(kernel, outs, scratch=(), flops=0, moved=0, **kw):
    return pl.pallas_call(
        kernel,
        out_shape=outs,
        scratch_shapes=list(scratch),
        compiler_params=pltpu.CompilerParams(vmem_limit_bytes=kw.pop("limit", 32) << 20),
        cost_estimate=pl.CostEstimate(flops=flops, bytes_accessed=moved, transcendentals=0),
        **kw,
    )


def whole():
    return pl.BlockSpec(memory_space=pltpu.VMEM)


def far():
    return pl.BlockSpec(memory_space=pltpu.HBM)


def struct(shape, dtype):
    return jax.ShapeDtypeStruct(shape, dtype)


def pack(og, li, rw, ids):
    return call(
        pack_kernel,
        struct((PEERS, CHUNK, WIDE), BF16),
        [pltpu.VMEM(a.shape, a.dtype) for a in (og, li, rw, ids)]
        + [pltpu.VMEM((PEERS, WIDE), F32)] * 2
        + [pltpu.SemaphoreType.DMA((4,))],
        flops=10**9,
        moved=2 * 10**6,
        in_specs=[far()] * 4,
        name="pack",
    )(og, li, rw, ids)


def expert(recv, w, h, perm):
    return call(
        expert_kernel,
        (struct((SLOTS, SLOTS), BF16), struct((PEERS * 4, 128), F32)),
        [pltpu.VMEM((SLOTS, PARTS * WIDE), BF16)],
        flops=12 * 10**8,
        moved=4 * 10**6,
        name="expert",
    )(recv, w, h, perm)


def side(recv, hg):
    return call(
        side_kernel,
        (
            struct((GROUPS, PEERS, 128), F32),
            struct((GROUPS, PEERS, 128), F32),
            struct(hg.shape, BF16),
        ),
        [pltpu.SemaphoreType.DMA],
        flops=10**8,
        moved=2 * 10**6,
        out_specs=(whole(), whole(), far()),
        name="side",
    )(recv, hg)


def logit_grads(me, s, code, gate):
    return call(
        logit_kernel,
        struct((PEERS, TOK), BF16),
        flops=10**6,
        moved=2 * 10**5,
        in_specs=[pl.BlockSpec(memory_space=pltpu.SMEM)] + [whole()] * 3,
        name="logits",
    )(me, s, code, gate)


def input_grads(lg, og, rw):
    return call(
        input_kernel,
        struct(og.shape, BF16),
        [pltpu.VMEM(a.shape, BF16) for a in (og, rw, og)] + [pltpu.SemaphoreType.DMA((9,))],
        flops=10**7,
        moved=10**6,
        in_specs=[whole(), far(), far()],
        out_specs=far(),
        name="inputs",
    )(lg, og, rw)


def router_grads(s, code, gate, recv, tie):
    return call(
        router_kernel,
        struct((TOK, PEERS), F32),
        [
            pltpu.VMEM((TOK, PEERS * TOK), F32),
            pltpu.VMEM((128, CAP * 128), BF16),
            pltpu.VMEM((PEERS, PEERS * TOK), BF16),
        ],
        flops=3 * 10**8,
        moved=2 * 10**6,
        name="router",
    )(s, code, gate, recv, tie)


def shifted(x):
    n = lax.axis_size("section")
    return lax.ppermute(x, "section", [(i, (i - 1) % n) for i in range(n)])


def exchange(x):
    return lax.all_to_all(x, "expert", split_axis=0, concat_axis=0, tiled=True)


def shards(out_grad, layer_input, router_weight, expert_ids, hidden_act, down_weight):
    og, li = out_grad[0], layer_input[0]
    rw = jnp.swapaxes(router_weight[0], 0, 1)
    ids = jnp.swapaxes(expert_ids[0], 0, 1)
    far_args = [pltpu.with_memory_space_constraint(a, pltpu.HBM) for a in (og, li, rw, ids)]
    me = lax.axis_index("expert").astype(jnp.int32).reshape(1)
    send = pack(*far_args)
    recv = exchange(send)
    hidden_near, sdg = expert(
        recv, down_weight[0, 0], hidden_act[0, 0], jnp.asarray(compaction(), BF16)
    )
    back = exchange(sdg.reshape(PEERS, 4, 128)).reshape(PEERS * 4, 128)
    og_held, rw_held, sdg = lax.optimization_barrier((og, rw, sdg))
    og_next, rw_next = shifted(og_held), shifted(rw_held)
    all_gate, all_code, hidden_grad = side(recv, hidden_near)
    logit_grad = logit_grads(me, back, all_code, all_gate)
    logit_next = shifted(logit_grad)
    router_grad = router_grads(back, all_code, all_gate, recv, logit_grad)
    sent = input_grads(logit_next, og_next, rw_next)[None]
    return sent, hidden_grad[None, None], router_grad[None]


def solution(mesh):
    placed = (
        P("section", "expert", None),
        P("section", "expert", None),
        P("section", None, None),
        P("section", "expert", None),
        P("section", "expert", None, None),
        P("section", "expert", None, None),
    )
    return jax.shard_map(
        shards,
        mesh=mesh,
        in_specs=placed,
        out_specs=(
            P("section", "expert", None),
            P("section", "expert", None, None),
            P("section", "expert", None),
        ),
        check_vma=False,
    )
```

```python
import jax
import jax.numpy as jnp
import numpy as np
from jax import lax
from jax.experimental import pallas as pl
from jax.experimental.pallas import tpu as pltpu
from jax.sharding import PartitionSpec as P

F32 = jnp.float32
BF16 = jnp.bfloat16
PEERS = 64
CAP = 6
TOK = 32
WIDE = 256
PARTS = 8
ROWS = PARTS * CAP
CHUNK = ROWS + 8
SLOTS = PEERS * CAP
GROUPS = 16


def dot(a, b, ca, cb):
    return lax.dot_general(a, b, (((ca,), (cb,)), ((), ())), preferred_element_type=F32)


def iota(shape, dim):
    return lax.broadcasted_iota(jnp.int32, shape, dim)


def compaction():
    p = np.zeros((4 * ROWS, 4 * ROWS), np.float32)
    for part in range(PARTS):
        for b in range(4):
            for c in range(CAP):
                p[part * 4 * CAP + b * CAP + c, b * ROWS + part * CAP + c] = 1
    return p


def spreading():
    row, lane = iota((128, CAP * 128), 0), iota((128, CAP * 128), 1)
    slot = ((lane // TOK) & 3) * CAP + lane // 128
    return jnp.where(((row & 31) == slot) & (row < 96), 1.0, 0.0).astype(BF16)


def pack_kernel(
    og_hbm, li_hbm, rw_hbm, ids_hbm, send_ref, og_ref, li_ref, rw_ref, ids_ref, gt_ref, ct_ref, sems
):
    pairs = ((ids_hbm, ids_ref), (rw_hbm, rw_ref), (li_hbm, li_ref), (og_hbm, og_ref))
    copies = [pltpu.make_async_copy(a, b, sems.at[i]) for i, (a, b) in enumerate(pairs)]
    for copy in copies:
        copy.start()
    copies[0].wait()
    ids = ids_ref[...]
    expert = iota((PEERS, TOK), 0)
    named = jnp.zeros((PEERS, TOK), F32)
    for k in range(8):
        named = jnp.where(ids[k : k + 1, :] == expert, 1.0, named)
    token = iota((TOK, WIDE), 0)
    lane = iota((TOK, WIDE), 1) & (TOK - 1)
    tile = jnp.where(token == lane, 1.0, 0.0).astype(BF16)
    ahead = jnp.where(token < lane, 1.0, 0.0).astype(BF16)
    named_b = named.astype(BF16)
    code = jnp.where(dot(named_b, tile, 1, 0) > 0.5, dot(named_b, ahead, 1, 0), -1.0)
    ct_ref[...] = code
    copies[1].wait()
    copies[2].wait()
    logits = dot(rw_ref[...], li_ref[...], 1, 1)
    weights = jnp.where(named > 0.5, jnp.exp(logits), 0.0)
    gates = (weights / jnp.sum(weights, axis=0, keepdims=True)).astype(BF16)
    gt_ref[...] = dot(gates, tile, 1, 0)
    gates_f = gates.astype(F32)

    choice = iota((8, TOK), 0)
    compact = jnp.zeros((8, TOK), F32)
    for k in range(8):
        one = jnp.sum(jnp.where(ids[k : k + 1, :] == expert, gates_f, 0.0), axis=0, keepdims=True)
        compact = jnp.where(choice == k, one, compact)
    t128, l128 = iota((TOK, 128), 0), iota((TOK, 128), 1)
    put_ids = jnp.where(t128 == l128, 1.0, 0.0).astype(BF16)
    put_gates = jnp.where(t128 + TOK == l128, 1.0, 0.0).astype(BF16)
    info = dot(ids.astype(F32).astype(BF16), put_ids, 1, 0) + dot(
        compact.astype(BF16), put_gates, 1, 0
    )
    send_ref[:, ROWS:, 128:] = jnp.broadcast_to(info.astype(BF16)[None], (PEERS, 8, 128))

    spread = dot(li_ref[...], tile[:, :128], 0, 0).reshape(PEERS, 4, 8, 128)
    quarter = iota((PEERS, 8, 128), 2) // TOK
    columns = spread[:, 0]
    for h in range(1, 4):
        columns = jnp.where(quarter == h, spread[:, h], columns)
    send_ref[:, ROWS:, :128] = columns.astype(BF16)

    copies[3].wait()
    stacked = jnp.concatenate(
        [og_ref[:, j * WIDE : (j + 1) * WIDE] for j in range(PARTS)], axis=0
    )
    row = iota((ROWS, WIDE), 0)
    part = jnp.zeros((ROWS, WIDE), jnp.int32)
    for j in range(1, PARTS):
        part = part + jnp.where(row >= j * CAP, 1, 0)
    slot = jnp.where(iota((ROWS, WIDE), 1) // TOK == part, row - part * CAP, -2).astype(F32)

    def step(i, carry):
        picks = []
        for u in range(8):
            at = pl.ds(i * 8 + u, 1)
            hit = jnp.broadcast_to(ct_ref[at, :], (ROWS, WIDE)) == slot
            picks.append(
                jnp.where(hit, jnp.broadcast_to(gt_ref[at, :], (ROWS, WIDE)), 0.0).astype(BF16)
            )
        rows = dot(jnp.concatenate(picks, axis=0), stacked, 1, 0).astype(BF16)
        send_ref[pl.ds(i * 8, 8), :ROWS, :] = rows.reshape(8, ROWS, WIDE)
        return carry

    lax.fori_loop(0, PEERS // 8, step, 0, unroll=8)


def expert_kernel(recv_ref, w_ref, h_ref, perm_ref, hg_ref, sdg_ref, rows_ref):
    perm = perm_ref[...]
    for g in range(8):
        halves = []
        for h in range(2):
            b = g * 8 + h * 4
            chunk = recv_ref[b : b + 4, :ROWS, :].reshape(4 * ROWS, WIDE)
            halves.append(dot(perm, chunk, 1, 0))
        for j in range(PARTS):
            piece = jnp.concatenate([m[j * 24 : (j + 1) * 24] for m in halves], axis=0)
            rows_ref[g * ROWS : (g + 1) * ROWS, j * WIDE : (j + 1) * WIDE] = piece.astype(BF16)
    grad = dot(rows_ref[...], w_ref[...], 1, 1)
    hg_ref[...] = grad.astype(BF16)
    prod = grad * h_ref[...].astype(F32)
    part = prod[:, :128] + prod[:, 128:256] + prod[:, 256:]
    gap = jnp.zeros((8, 128), F32)
    pieces = []
    for g in range(GROUPS):
        pieces += [part[g * 24 : (g + 1) * 24], gap]
    padded = jnp.concatenate(pieces, axis=0)
    line = jnp.sum(padded.T, axis=0, keepdims=True)
    which = iota((8, 128), 0) & 3
    out = jnp.zeros((8, 128), F32)
    for t in range(4):
        out = jnp.where(which == t, line[:, t * 128 : (t + 1) * 128], out)
    sdg_ref[...] = jnp.broadcast_to(out[None], (PEERS // 2, 8, 128)).reshape(PEERS * 4, 128)


def gather(blocks, at):
    quarter = iota((8, 128), 1) // TOK
    out = None
    for i, block in enumerate(blocks):
        shift = (i - at) * TOK % 128
        moved = pltpu.roll(block, shift, axis=1) if shift else block
        out = moved if out is None else jnp.where(quarter == i, moved, out)
    return out


def side_kernel(recv_ref, hg_ref, gate_ref, code_ref, hg_hbm, sem):
    copy = pltpu.make_async_copy(hg_ref, hg_hbm, sem)
    copy.start()
    expert = iota((PEERS, 128), 0).astype(F32)
    row, col = iota((128, 128), 0), iota((128, 128), 1)
    ahead = jnp.where((row // TOK == col // TOK) & (row < col), 1.0, 0.0).astype(BF16)
    for g in range(GROUPS):
        info = [recv_ref[4 * g + i, ROWS:, 128:].astype(F32) for i in range(4)]
        ids, gates = gather(info, 0), gather(info, 1)
        named = jnp.zeros((PEERS, 128), F32)
        dense = jnp.zeros((PEERS, 128), F32)
        for k in range(8):
            hit = ids[k : k + 1, :] == expert
            named = jnp.where(hit, 1.0, named)
            dense = jnp.where(hit, gates[k : k + 1, :], dense)
        rank = dot(named.astype(BF16), ahead, 1, 0)
        code_ref[g] = jnp.where(named > 0.5, rank, -1.0).astype(BF16)
        gate_ref[g] = dense.astype(BF16)
    copy.wait()


def logit_kernel(me_ref, s_ref, code_ref, gate_ref, out_ref):
    me = me_ref[0]
    mine = s_ref[pl.ds(me // 16, PEERS, stride=4), :]
    offset = ((me // 4) % 4) * 32 + (me % 4) * CAP
    mine = pltpu.roll(mine, (128 - offset) % 128, axis=1)
    back = (128 - (me % 4) * TOK) % 128
    code = pltpu.roll(code_ref[me // 4].astype(F32), back, axis=1)[:, :TOK]
    gate = pltpu.roll(gate_ref[me // 4].astype(F32), back, axis=1)[:, :TOK]
    sdg = jnp.zeros((PEERS, TOK), F32)
    for c in range(CAP):
        sdg = jnp.where(code == c, mine[:, c : c + 1], sdg)
    total = jnp.sum(sdg, axis=0, keepdims=True)
    out_ref[...] = (sdg - gate * total).astype(BF16)


def input_kernel(lg_ref, og_ref, rw_ref, out_hbm, out_ref, sems):
    lg = lg_ref[...]
    copies = []
    for i in range(2):
        at = pl.ds(i * 1024, 1024)
        part = dot(lg, rw_ref[:, at], 0, 0)
        out_ref[:, at] = (og_ref[:, at].astype(F32) + part).astype(BF16)
        copies.append(pltpu.make_async_copy(out_ref.at[:, at], out_hbm.at[:, at], sems.at[i]))
        copies[i].start()
    for copy in copies:
        copy.wait()


def router_kernel(
    s_ref, code_ref, gate_ref, recv_ref, tie_ref, out_ref, cols_ref, spread_ref, lg_ref
):
    del tie_ref
    spread_ref[...] = spreading()
    for g in range(GROUPS):
        cols = [recv_ref[4 * g + i, ROWS:, :128].astype(F32) for i in range(4)]
        for h in range(4):
            cols_ref[h * 8 : (h + 1) * 8, g * 128 : (g + 1) * 128] = gather(cols, h)
    lane = iota((PEERS, 128), 1)
    for t in range(4):
        tile = s_ref[pl.ds(t, PEERS, stride=4), :]
        for q in range(4):
            g = t * 4 + q
            x = pltpu.roll(tile, 128 - 32 * q, axis=1) if q else tile
            x = jnp.where(lane < 24, x, 0.0)
            hi = x.astype(BF16).astype(F32)
            rest = x - hi
            mid = rest.astype(BF16).astype(F32)
            low = (rest - mid).astype(BF16).astype(F32)
            z = hi + pltpu.roll(mid, 32, axis=1) + pltpu.roll(low, 64, axis=1)
            wide = dot(z.astype(BF16), spread_ref[...], 1, 0)
            code = code_ref[g].astype(F32)
            sdg = jnp.zeros((PEERS, 128), F32)
            for c in range(CAP):
                sdg = jnp.where(code == c, wide[:, c * 128 : (c + 1) * 128], sdg)
            total = jnp.sum(sdg, axis=0, keepdims=True)
            lg_ref[:, g * 128 : (g + 1) * 128] = (sdg - gate_ref[g].astype(F32) * total).astype(BF16)
    out_ref[...] = dot(cols_ref[...].astype(BF16), lg_ref[...], 1, 1)


def call(kernel, outs, scratch=(), flops=0, moved=0, **kw):
    return pl.pallas_call(
        kernel,
        out_shape=outs,
        scratch_shapes=list(scratch),
        compiler_params=pltpu.CompilerParams(vmem_limit_bytes=kw.pop("limit", 32) << 20),
        cost_estimate=pl.CostEstimate(flops=flops, bytes_accessed=moved, transcendentals=0),
        **kw,
    )


def whole():
    return pl.BlockSpec(memory_space=pltpu.VMEM)


def far():
    return pl.BlockSpec(memory_space=pltpu.HBM)


def struct(shape, dtype):
    return jax.ShapeDtypeStruct(shape, dtype)


def pack(og, li, rw, ids):
    return call(
        pack_kernel,
        struct((PEERS, CHUNK, WIDE), BF16),
        [pltpu.VMEM(a.shape, a.dtype) for a in (og, li, rw, ids)]
        + [pltpu.VMEM((PEERS, WIDE), F32)] * 2
        + [pltpu.SemaphoreType.DMA((4,))],
        flops=10**9,
        moved=2 * 10**6,
        in_specs=[far()] * 4,
        name="pack",
    )(og, li, rw, ids)


def expert(recv, w, h, perm):
    return call(
        expert_kernel,
        (struct((SLOTS, SLOTS), BF16), struct((PEERS * 4, 128), F32)),
        [pltpu.VMEM((SLOTS, PARTS * WIDE), BF16)],
        flops=12 * 10**8,
        moved=4 * 10**6,
        name="expert",
    )(recv, w, h, perm)


def side(recv, hg):
    return call(
        side_kernel,
        (
            struct((GROUPS, PEERS, 128), BF16),
            struct((GROUPS, PEERS, 128), BF16),
            struct(hg.shape, BF16),
        ),
        [pltpu.SemaphoreType.DMA],
        flops=10**8,
        moved=2 * 10**6,
        out_specs=(whole(), whole(), far()),
        name="side",
    )(recv, hg)


def logit_grads(me, s, code, gate):
    return call(
        logit_kernel,
        struct((PEERS, TOK), BF16),
        flops=10**6,
        moved=2 * 10**5,
        in_specs=[pl.BlockSpec(memory_space=pltpu.SMEM)] + [whole()] * 3,
        name="logits",
    )(me, s, code, gate)


def input_grads(lg, og, rw):
    return call(
        input_kernel,
        struct(og.shape, BF16),
        [pltpu.VMEM(og.shape, BF16), pltpu.SemaphoreType.DMA((2,))],
        flops=10**7,
        moved=10**6,
        out_specs=far(),
        name="inputs",
    )(lg, og, rw)


def router_grads(s, code, gate, recv, tie):
    return call(
        router_kernel,
        struct((TOK, PEERS), F32),
        [
            pltpu.VMEM((TOK, PEERS * TOK), F32),
            pltpu.VMEM((128, CAP * 128), BF16),
            pltpu.VMEM((PEERS, PEERS * TOK), BF16),
        ],
        flops=3 * 10**8,
        moved=2 * 10**6,
        name="router",
    )(s, code, gate, recv, tie)


def shifted(x):
    n = lax.axis_size("section")
    return lax.ppermute(x, "section", [(i, (i - 1) % n) for i in range(n)])


def exchange(x):
    return lax.all_to_all(x, "expert", split_axis=0, concat_axis=0, tiled=True)


def shards(out_grad, layer_input, router_weight, expert_ids, hidden_act, down_weight):
    og, li = out_grad[0], layer_input[0]
    rw = jnp.swapaxes(router_weight[0], 0, 1)
    ids = jnp.swapaxes(expert_ids[0], 0, 1)
    far_args = [pltpu.with_memory_space_constraint(a, pltpu.HBM) for a in (og, li, rw, ids)]
    me = lax.axis_index("expert").astype(jnp.int32).reshape(1)
    send = pack(*far_args)
    recv = exchange(send)
    hidden_near, sdg = expert(
        recv, down_weight[0, 0], hidden_act[0, 0], jnp.asarray(compaction(), BF16)
    )
    back = exchange(sdg.reshape(PEERS, 4, 128)).reshape(PEERS * 4, 128)
    og_held, rw_held, sdg = lax.optimization_barrier((og, rw, sdg))
    og_next, rw_next = shifted(og_held), shifted(rw_held)
    all_gate, all_code, hidden_grad = side(recv, hidden_near)
    logit_grad = logit_grads(me, back, all_code, all_gate)
    logit_next = shifted(logit_grad)
    router_grad = router_grads(back, all_code, all_gate, recv, logit_grad)
    sent = input_grads(logit_next, og_next, rw_next)[None]
    return sent, hidden_grad[None, None], router_grad[None]


def solution(mesh):
    placed = (
        P("section", "expert", None),
        P("section", "expert", None),
        P("section", None, None),
        P("section", "expert", None),
        P("section", "expert", None, None),
        P("section", "expert", None, None),
    )
    return jax.shard_map(
        shards,
        mesh=mesh,
        in_specs=placed,
        out_specs=(
            P("section", "expert", None),
            P("section", "expert", None, None),
            P("section", "expert", None),
        ),
        check_vma=False,
    )
```

```python
import jax
import jax.numpy as jnp
import numpy as np
from jax import lax
from jax.experimental import pallas as pl
from jax.experimental.pallas import tpu as pltpu
from jax.sharding import PartitionSpec as P

F32 = jnp.float32
BF16 = jnp.bfloat16
PEERS = 64
CAP = 6
TOK = 32
WIDE = 256
PARTS = 8
ROWS = PARTS * CAP
CHUNK = ROWS + 8
SLOTS = PEERS * CAP
GROUPS = 16


def dot(a, b, ca, cb):
    return lax.dot_general(a, b, (((ca,), (cb,)), ((), ())), preferred_element_type=F32)


def iota(shape, dim):
    return lax.broadcasted_iota(jnp.int32, shape, dim)


def compaction():
    p = np.zeros((4 * ROWS, 4 * ROWS), np.float32)
    for part in range(PARTS):
        for b in range(4):
            for c in range(CAP):
                p[part * 4 * CAP + b * CAP + c, b * ROWS + part * CAP + c] = 1
    return p


def spreading():
    row, lane = iota((128, CAP * 128), 0), iota((128, CAP * 128), 1)
    slot = ((lane // TOK) & 3) * CAP + lane // 128
    return jnp.where(((row & 31) == slot) & (row < 96), 1.0, 0.0).astype(BF16)


def pack_kernel(
    og_hbm, li_hbm, rw_hbm, ids_hbm, send_ref, og_ref, li_ref, rw_ref, ids_ref, gt_ref, ct_ref, sems
):
    pairs = ((ids_hbm, ids_ref), (rw_hbm, rw_ref), (li_hbm, li_ref), (og_hbm, og_ref))
    copies = [pltpu.make_async_copy(a, b, sems.at[i]) for i, (a, b) in enumerate(pairs)]
    for copy in copies:
        copy.start()
    copies[0].wait()
    ids = ids_ref[...]
    expert = iota((PEERS, TOK), 0)
    named = jnp.zeros((PEERS, TOK), F32)
    for k in range(8):
        named = jnp.where(ids[k : k + 1, :] == expert, 1.0, named)
    token = iota((TOK, WIDE), 0)
    lane = iota((TOK, WIDE), 1) & (TOK - 1)
    tile = jnp.where(token == lane, 1.0, 0.0).astype(BF16)
    ahead = jnp.where(token < lane, 1.0, 0.0).astype(BF16)
    named_b = named.astype(BF16)
    code = jnp.where(dot(named_b, tile, 1, 0) > 0.5, dot(named_b, ahead, 1, 0), -1.0)
    ct_ref[...] = code
    copies[1].wait()
    copies[2].wait()
    logits = dot(rw_ref[...], li_ref[...], 1, 1)
    weights = jnp.where(named > 0.5, jnp.exp(logits), 0.0)
    gates = (weights / jnp.sum(weights, axis=0, keepdims=True)).astype(BF16)
    gt_ref[...] = dot(gates, tile, 1, 0)
    gates_f = gates.astype(F32)

    choice = iota((8, TOK), 0)
    compact = jnp.zeros((8, TOK), F32)
    for k in range(8):
        one = jnp.sum(jnp.where(ids[k : k + 1, :] == expert, gates_f, 0.0), axis=0, keepdims=True)
        compact = jnp.where(choice == k, one, compact)
    t128, l128 = iota((TOK, 128), 0), iota((TOK, 128), 1)
    put_ids = jnp.where(t128 == l128, 1.0, 0.0).astype(BF16)
    put_gates = jnp.where(t128 + TOK == l128, 1.0, 0.0).astype(BF16)
    info = dot(ids.astype(F32).astype(BF16), put_ids, 1, 0) + dot(
        compact.astype(BF16), put_gates, 1, 0
    )
    send_ref[:, ROWS:, 128:] = jnp.broadcast_to(info.astype(BF16)[None], (PEERS, 8, 128))

    spread = dot(li_ref[...], tile[:, :128], 0, 0).reshape(PEERS, 4, 8, 128)
    quarter = iota((PEERS, 8, 128), 2) // TOK
    columns = spread[:, 0]
    for h in range(1, 4):
        columns = jnp.where(quarter == h, spread[:, h], columns)
    send_ref[:, ROWS:, :128] = columns.astype(BF16)

    copies[3].wait()
    stacked = jnp.concatenate(
        [og_ref[:, j * WIDE : (j + 1) * WIDE] for j in range(PARTS)], axis=0
    )
    row = iota((ROWS, WIDE), 0)
    part = jnp.zeros((ROWS, WIDE), jnp.int32)
    for j in range(1, PARTS):
        part = part + jnp.where(row >= j * CAP, 1, 0)
    slot = jnp.where(iota((ROWS, WIDE), 1) // TOK == part, row - part * CAP, -2).astype(F32)

    def step(i, carry):
        picks = []
        for u in range(8):
            at = pl.ds(i * 8 + u, 1)
            hit = jnp.broadcast_to(ct_ref[at, :], (ROWS, WIDE)) == slot
            picks.append(
                jnp.where(hit, jnp.broadcast_to(gt_ref[at, :], (ROWS, WIDE)), 0.0).astype(BF16)
            )
        rows = dot(jnp.concatenate(picks, axis=0), stacked, 1, 0).astype(BF16)
        send_ref[pl.ds(i * 8, 8), :ROWS, :] = rows.reshape(8, ROWS, WIDE)
        return carry

    lax.fori_loop(0, PEERS // 8, step, 0, unroll=8)


def expert_kernel(recv_ref, w_ref, h_ref, perm_ref, hg_ref, sdg_ref, rows_ref):
    perm = perm_ref[...]
    for g in range(8):
        halves = []
        for h in range(2):
            b = g * 8 + h * 4
            chunk = recv_ref[b : b + 4, :ROWS, :].reshape(4 * ROWS, WIDE)
            halves.append(dot(perm, chunk, 1, 0))
        for j in range(PARTS):
            piece = jnp.concatenate([m[j * 24 : (j + 1) * 24] for m in halves], axis=0)
            rows_ref[g * ROWS : (g + 1) * ROWS, j * WIDE : (j + 1) * WIDE] = piece.astype(BF16)
    grad = dot(rows_ref[...], w_ref[...], 1, 1)
    hg_ref[...] = grad.astype(BF16)
    prod = grad * h_ref[...].astype(F32)
    part = prod[:, :128] + prod[:, 128:256] + prod[:, 256:]
    line = jnp.sum(part.T, axis=0, keepdims=True)
    row = iota((24, 128), 0)
    which = row - 3 * ((row.astype(F32) + 0.5) * (1 / 3)).astype(jnp.int32)
    out = jnp.zeros((24, 128), F32)
    for t in range(3):
        out = jnp.where(which == t, line[:, t * 128 : (t + 1) * 128], out)
    sdg_ref[...] = jnp.broadcast_to(out[None], (8, 24, 128)).reshape(PEERS * 3, 128)


def gather(blocks, at):
    quarter = iota((8, 128), 1) // TOK
    out = None
    for i, block in enumerate(blocks):
        shift = (i - at) * TOK % 128
        moved = pltpu.roll(block, shift, axis=1) if shift else block
        out = moved if out is None else jnp.where(quarter == i, moved, out)
    return out


def side_kernel(recv_ref, hg_ref, gate_ref, code_ref, hg_hbm, sem):
    copy = pltpu.make_async_copy(hg_ref, hg_hbm, sem)
    copy.start()
    expert = iota((PEERS, 128), 0).astype(F32)
    row, col = iota((128, 128), 0), iota((128, 128), 1)
    ahead = jnp.where((row // TOK == col // TOK) & (row < col), 1.0, 0.0).astype(BF16)
    for g in range(GROUPS):
        info = [recv_ref[4 * g + i, ROWS:, 128:].astype(F32) for i in range(4)]
        ids, gates = gather(info, 0), gather(info, 1)
        named = jnp.zeros((PEERS, 128), F32)
        dense = jnp.zeros((PEERS, 128), F32)
        for k in range(8):
            hit = ids[k : k + 1, :] == expert
            named = jnp.where(hit, 1.0, named)
            dense = jnp.where(hit, gates[k : k + 1, :], dense)
        rank = dot(named.astype(BF16), ahead, 1, 0)
        code_ref[g] = jnp.where(named > 0.5, rank, -1.0).astype(BF16)
        gate_ref[g] = dense.astype(BF16)
    copy.wait()


def logit_kernel(me_ref, s_ref, code_ref, gate_ref, out_ref):
    me = me_ref[0]
    tile, offset = me * CAP // 128, me * CAP % 128
    mine, after = [
        pltpu.roll(s_ref[pl.ds(t, PEERS, stride=3), :], (128 - offset) % 128, axis=1)
        for t in (tile, jnp.minimum(tile + 1, 2))
    ]
    mine = jnp.where(iota((PEERS, 128), 1) < 128 - offset, mine, after)
    back = (128 - (me % 4) * TOK) % 128
    code = pltpu.roll(code_ref[me // 4].astype(F32), back, axis=1)[:, :TOK]
    gate = pltpu.roll(gate_ref[me // 4].astype(F32), back, axis=1)[:, :TOK]
    sdg = jnp.zeros((PEERS, TOK), F32)
    for c in range(CAP):
        sdg = jnp.where(code == c, mine[:, c : c + 1], sdg)
    total = jnp.sum(sdg, axis=0, keepdims=True)
    out_ref[...] = (sdg - gate * total).astype(BF16)


def input_kernel(lg_ref, og_ref, rw_ref, out_hbm, out_ref, sems):
    lg = lg_ref[...]
    copies = []
    for i in range(2):
        at = pl.ds(i * 1024, 1024)
        part = dot(lg, rw_ref[:, at], 0, 0)
        out_ref[:, at] = (og_ref[:, at].astype(F32) + part).astype(BF16)
        copies.append(pltpu.make_async_copy(out_ref.at[:, at], out_hbm.at[:, at], sems.at[i]))
        copies[i].start()
    for copy in copies:
        copy.wait()


def router_kernel(
    s_ref, code_ref, gate_ref, recv_ref, tie_ref, out_ref, cols_ref, spread_ref, lg_ref
):
    del tie_ref
    spread_ref[...] = spreading()
    for g in range(GROUPS):
        cols = [recv_ref[4 * g + i, ROWS:, :128].astype(F32) for i in range(4)]
        for h in range(4):
            cols_ref[h * 8 : (h + 1) * 8, g * 128 : (g + 1) * 128] = gather(cols, h)
    lane = iota((PEERS, 128), 1)
    tiles = [s_ref[pl.ds(t, PEERS, stride=3), :] for t in range(3)]
    for g in range(GROUPS):
        t, offset = g * 24 // 128, g * 24 % 128
        x = pltpu.roll(tiles[t], 128 - offset, axis=1) if offset else tiles[t]
        if offset + 24 > 128:
            x = jnp.where(lane < 128 - offset, x, pltpu.roll(tiles[t + 1], 128 - offset, axis=1))
        x = jnp.where(lane < 24, x, 0.0)
        hi = x.astype(BF16).astype(F32)
        rest = x - hi
        mid = rest.astype(BF16).astype(F32)
        low = (rest - mid).astype(BF16).astype(F32)
        z = hi + pltpu.roll(mid, 32, axis=1) + pltpu.roll(low, 64, axis=1)
        wide = dot(z.astype(BF16), spread_ref[...], 1, 0)
        code = code_ref[g].astype(F32)
        sdg = jnp.zeros((PEERS, 128), F32)
        for c in range(CAP):
            sdg = jnp.where(code == c, wide[:, c * 128 : (c + 1) * 128], sdg)
        total = jnp.sum(sdg, axis=0, keepdims=True)
        lg_ref[:, g * 128 : (g + 1) * 128] = (sdg - gate_ref[g].astype(F32) * total).astype(BF16)
    out_ref[...] = dot(cols_ref[...].astype(BF16), lg_ref[...], 1, 1)


def call(kernel, outs, scratch=(), flops=0, moved=0, **kw):
    return pl.pallas_call(
        kernel,
        out_shape=outs,
        scratch_shapes=list(scratch),
        compiler_params=pltpu.CompilerParams(vmem_limit_bytes=kw.pop("limit", 32) << 20),
        cost_estimate=pl.CostEstimate(flops=flops, bytes_accessed=moved, transcendentals=0),
        **kw,
    )


def whole():
    return pl.BlockSpec(memory_space=pltpu.VMEM)


def far():
    return pl.BlockSpec(memory_space=pltpu.HBM)


def struct(shape, dtype):
    return jax.ShapeDtypeStruct(shape, dtype)


def pack(og, li, rw, ids):
    return call(
        pack_kernel,
        struct((PEERS, CHUNK, WIDE), BF16),
        [pltpu.VMEM(a.shape, a.dtype) for a in (og, li, rw, ids)]
        + [pltpu.VMEM((PEERS, WIDE), F32)] * 2
        + [pltpu.SemaphoreType.DMA((4,))],
        flops=10**9,
        moved=2 * 10**6,
        in_specs=[far()] * 4,
        name="pack",
    )(og, li, rw, ids)


def expert(recv, w, h, perm):
    return call(
        expert_kernel,
        (struct((SLOTS, SLOTS), BF16), struct((PEERS * 3, 128), F32)),
        [pltpu.VMEM((SLOTS, PARTS * WIDE), BF16)],
        flops=12 * 10**8,
        moved=4 * 10**6,
        name="expert",
    )(recv, w, h, perm)


def side(recv, hg):
    return call(
        side_kernel,
        (
            struct((GROUPS, PEERS, 128), BF16),
            struct((GROUPS, PEERS, 128), BF16),
            struct(hg.shape, BF16),
        ),
        [pltpu.SemaphoreType.DMA],
        flops=10**8,
        moved=2 * 10**6,
        out_specs=(whole(), whole(), far()),
        name="side",
    )(recv, hg)


def logit_grads(me, s, code, gate):
    return call(
        logit_kernel,
        struct((PEERS, TOK), BF16),
        flops=10**6,
        moved=2 * 10**5,
        in_specs=[pl.BlockSpec(memory_space=pltpu.SMEM)] + [whole()] * 3,
        name="logits",
    )(me, s, code, gate)


def input_grads(lg, og, rw):
    return call(
        input_kernel,
        struct(og.shape, BF16),
        [pltpu.VMEM(og.shape, BF16), pltpu.SemaphoreType.DMA((2,))],
        flops=10**7,
        moved=10**6,
        out_specs=far(),
        name="inputs",
    )(lg, og, rw)


def router_grads(s, code, gate, recv, tie):
    return call(
        router_kernel,
        struct((TOK, PEERS), F32),
        [
            pltpu.VMEM((TOK, PEERS * TOK), F32),
            pltpu.VMEM((128, CAP * 128), BF16),
            pltpu.VMEM((PEERS, PEERS * TOK), BF16),
        ],
        flops=10**9,
        moved=2 * 10**6,
        name="router",
    )(s, code, gate, recv, tie)


def shifted(x):
    n = lax.axis_size("section")
    return lax.ppermute(x, "section", [(i, (i - 1) % n) for i in range(n)])


def exchange(x):
    return lax.all_to_all(x, "expert", split_axis=0, concat_axis=0, tiled=True)


def shards(out_grad, layer_input, router_weight, expert_ids, hidden_act, down_weight):
    og, li = out_grad[0], layer_input[0]
    rw = jnp.swapaxes(router_weight[0], 0, 1)
    ids = jnp.swapaxes(expert_ids[0], 0, 1)
    far_args = [pltpu.with_memory_space_constraint(a, pltpu.HBM) for a in (og, li, rw, ids)]
    me = lax.axis_index("expert").astype(jnp.int32).reshape(1)
    send = pack(*far_args)
    recv = exchange(send)
    hidden_near, sdg = expert(
        recv, down_weight[0, 0], hidden_act[0, 0], jnp.asarray(compaction(), BF16)
    )
    back = exchange(sdg.reshape(PEERS, 1, SLOTS)).reshape(PEERS * 3, 128)
    og_held, rw_held, sdg = lax.optimization_barrier((og, rw, sdg))
    og_next, rw_next = shifted(og_held), shifted(rw_held)
    all_gate, all_code, hidden_grad = side(recv, hidden_near)
    logit_grad = logit_grads(me, back, all_code, all_gate)
    logit_next = shifted(logit_grad)
    router_grad = router_grads(back, all_code, all_gate, recv, logit_grad)
    sent = input_grads(logit_next, og_next, rw_next)[None]
    return sent, hidden_grad[None, None], router_grad[None]


def solution(mesh):
    placed = (
        P("section", "expert", None),
        P("section", "expert", None),
        P("section", None, None),
        P("section", "expert", None),
        P("section", "expert", None, None),
        P("section", "expert", None, None),
    )
    return jax.shard_map(
        shards,
        mesh=mesh,
        in_specs=placed,
        out_specs=(
            P("section", "expert", None),
            P("section", "expert", None, None),
            P("section", "expert", None),
        ),
        check_vma=False,
    )
```

```python
import jax
import jax.numpy as jnp
import numpy as np
from jax import lax
from jax.experimental import pallas as pl
from jax.experimental.pallas import tpu as pltpu
from jax.sharding import PartitionSpec as P

F32 = jnp.float32
BF16 = jnp.bfloat16
PEERS = 64
CAP = 6
TOK = 32
WIDE = 256
PARTS = 8
ROWS = PARTS * CAP
CHUNK = ROWS + 8
SLOTS = PEERS * CAP
GROUPS = 16


def dot(a, b, ca, cb):
    return lax.dot_general(a, b, (((ca,), (cb,)), ((), ())), preferred_element_type=F32)


def iota(shape, dim):
    return lax.broadcasted_iota(jnp.int32, shape, dim)


def compaction():
    p = np.zeros((4 * ROWS, 4 * ROWS), np.float32)
    for part in range(PARTS):
        for b in range(4):
            for c in range(CAP):
                p[part * 4 * CAP + b * CAP + c, b * ROWS + part * CAP + c] = 1
    return p


def spreading():
    row, lane = iota((128, CAP * 128), 0), iota((128, CAP * 128), 1)
    slot = ((lane // TOK) & 3) * CAP + lane // 128
    return jnp.where(((row & 31) == slot) & (row < 96), 1.0, 0.0).astype(BF16)


def pack_kernel(
    og_hbm, li_hbm, rw_hbm, ids_hbm, send_ref, near_hbm,
    og_ref, li_ref, rw_ref, ids_ref, gt_ref, ct_ref, sems,
):
    pairs = ((ids_hbm, ids_ref), (rw_hbm, rw_ref), (li_hbm, li_ref), (og_hbm, og_ref))
    copies = [pltpu.make_async_copy(a, b, sems.at[i]) for i, (a, b) in enumerate(pairs)]
    for copy in copies:
        copy.start()
    joins = [
        pltpu.make_async_copy(og_hbm, near_hbm.at[pl.ds(0, TOK)], sems.at[4]),
        pltpu.make_async_copy(rw_hbm, near_hbm.at[pl.ds(TOK, PEERS)], sems.at[5]),
    ]
    for copy in joins:
        copy.start()
    copies[0].wait()
    ids = ids_ref[...]
    expert = iota((PEERS, TOK), 0)
    named = jnp.zeros((PEERS, TOK), F32)
    for k in range(8):
        named = jnp.where(ids[k : k + 1, :] == expert, 1.0, named)
    token = iota((TOK, WIDE), 0)
    lane = iota((TOK, WIDE), 1) & (TOK - 1)
    tile = jnp.where(token == lane, 1.0, 0.0).astype(BF16)
    ahead = jnp.where(token < lane, 1.0, 0.0).astype(BF16)
    named_b = named.astype(BF16)
    code = jnp.where(dot(named_b, tile, 1, 0) > 0.5, dot(named_b, ahead, 1, 0), -1.0)
    ct_ref[...] = code
    copies[1].wait()
    copies[2].wait()
    logits = dot(rw_ref[...], li_ref[...], 1, 1)
    weights = jnp.where(named > 0.5, jnp.exp(logits), 0.0)
    gates = (weights / jnp.sum(weights, axis=0, keepdims=True)).astype(BF16)
    gt_ref[...] = dot(gates, tile, 1, 0)
    gates_f = gates.astype(F32)

    choice = iota((8, TOK), 0)
    compact = jnp.zeros((8, TOK), F32)
    for k in range(8):
        one = jnp.sum(jnp.where(ids[k : k + 1, :] == expert, gates_f, 0.0), axis=0, keepdims=True)
        compact = jnp.where(choice == k, one, compact)
    t128, l128 = iota((TOK, 128), 0), iota((TOK, 128), 1)
    put_ids = jnp.where(t128 == l128, 1.0, 0.0).astype(BF16)
    put_gates = jnp.where(t128 + TOK == l128, 1.0, 0.0).astype(BF16)
    info = dot(ids.astype(F32).astype(BF16), put_ids, 1, 0) + dot(
        compact.astype(BF16), put_gates, 1, 0
    )
    send_ref[:, ROWS:, 128:] = jnp.broadcast_to(info.astype(BF16)[None], (PEERS, 8, 128))

    spread = dot(li_ref[...], tile[:, :128], 0, 0).reshape(PEERS, 4, 8, 128)
    quarter = iota((PEERS, 8, 128), 2) // TOK
    columns = spread[:, 0]
    for h in range(1, 4):
        columns = jnp.where(quarter == h, spread[:, h], columns)
    send_ref[:, ROWS:, :128] = columns.astype(BF16)

    copies[3].wait()
    stacked = jnp.concatenate(
        [og_ref[:, j * WIDE : (j + 1) * WIDE] for j in range(PARTS)], axis=0
    )
    row = iota((ROWS, WIDE), 0)
    part = jnp.zeros((ROWS, WIDE), jnp.int32)
    for j in range(1, PARTS):
        part = part + jnp.where(row >= j * CAP, 1, 0)
    slot = jnp.where(iota((ROWS, WIDE), 1) // TOK == part, row - part * CAP, -2).astype(F32)

    def step(i, carry):
        picks = []
        for u in range(8):
            at = pl.ds(i * 8 + u, 1)
            hit = jnp.broadcast_to(ct_ref[at, :], (ROWS, WIDE)) == slot
            picks.append(
                jnp.where(hit, jnp.broadcast_to(gt_ref[at, :], (ROWS, WIDE)), 0.0).astype(BF16)
            )
        rows = dot(jnp.concatenate(picks, axis=0), stacked, 1, 0).astype(BF16)
        send_ref[pl.ds(i * 8, 8), :ROWS, :] = rows.reshape(8, ROWS, WIDE)
        return carry

    lax.fori_loop(0, PEERS // 8, step, 0, unroll=8)
    for copy in joins:
        copy.wait()


def expert_kernel(recv_ref, w_ref, h_ref, perm_ref, hg_ref, sdg_ref, rows_ref):
    perm = perm_ref[...]
    for g in range(8):
        halves = []
        for h in range(2):
            b = g * 8 + h * 4
            chunk = recv_ref[b : b + 4, :ROWS, :].reshape(4 * ROWS, WIDE)
            halves.append(dot(perm, chunk, 1, 0))
        for j in range(PARTS):
            piece = jnp.concatenate([m[j * 24 : (j + 1) * 24] for m in halves], axis=0)
            rows_ref[g * ROWS : (g + 1) * ROWS, j * WIDE : (j + 1) * WIDE] = piece.astype(BF16)
    grad = dot(rows_ref[...], w_ref[...], 1, 1)
    hg_ref[...] = grad.astype(BF16)
    prod = grad * h_ref[...].astype(F32)
    part = prod[:, :128] + prod[:, 128:256] + prod[:, 256:]
    line = jnp.sum(part.T, axis=0, keepdims=True)
    row = iota((24, 128), 0)
    which = row - 3 * ((row.astype(F32) + 0.5) * (1 / 3)).astype(jnp.int32)
    out = jnp.zeros((24, 128), F32)
    for t in range(3):
        out = jnp.where(which == t, line[:, t * 128 : (t + 1) * 128], out)
    sdg_ref[...] = jnp.broadcast_to(out[None], (8, 24, 128)).reshape(PEERS * 3, 128)


def gather(blocks, at):
    quarter = iota((8, 128), 1) // TOK
    out = None
    for i, block in enumerate(blocks):
        shift = (i - at) * TOK % 128
        moved = pltpu.roll(block, shift, axis=1) if shift else block
        out = moved if out is None else jnp.where(quarter == i, moved, out)
    return out


def side_kernel(recv_ref, hg_ref, gate_ref, code_ref, hg_hbm, sem):
    copy = pltpu.make_async_copy(hg_ref, hg_hbm, sem)
    copy.start()
    expert = iota((PEERS, 128), 0).astype(F32)
    row, col = iota((128, 128), 0), iota((128, 128), 1)
    ahead = jnp.where((row // TOK == col // TOK) & (row < col), 1.0, 0.0).astype(BF16)
    for g in range(GROUPS):
        info = [recv_ref[4 * g + i, ROWS:, 128:].astype(F32) for i in range(4)]
        ids, gates = gather(info, 0), gather(info, 1)
        named = jnp.zeros((PEERS, 128), F32)
        dense = jnp.zeros((PEERS, 128), F32)
        for k in range(8):
            hit = ids[k : k + 1, :] == expert
            named = jnp.where(hit, 1.0, named)
            dense = jnp.where(hit, gates[k : k + 1, :], dense)
        rank = dot(named.astype(BF16), ahead, 1, 0)
        code_ref[g] = jnp.where(named > 0.5, rank, -1.0).astype(BF16)
        gate_ref[g] = dense.astype(BF16)
    copy.wait()


def logit_kernel(me_ref, s_ref, code_ref, gate_ref, out_ref):
    me = me_ref[0]
    tile, offset = me * CAP // 128, me * CAP % 128
    mine, after = [
        pltpu.roll(s_ref[pl.ds(t, PEERS, stride=3), :], (128 - offset) % 128, axis=1)
        for t in (tile, jnp.minimum(tile + 1, 2))
    ]
    mine = jnp.where(iota((PEERS, 128), 1) < 128 - offset, mine, after)
    back = (128 - (me % 4) * TOK) % 128
    code = pltpu.roll(code_ref[me // 4].astype(F32), back, axis=1)[:, :TOK]
    gate = pltpu.roll(gate_ref[me // 4].astype(F32), back, axis=1)[:, :TOK]
    sdg = jnp.zeros((PEERS, TOK), F32)
    for c in range(CAP):
        sdg = jnp.where(code == c, mine[:, c : c + 1], sdg)
    total = jnp.sum(sdg, axis=0, keepdims=True)
    out_ref[...] = (sdg - gate * total).astype(BF16)


def input_kernel(lg_ref, near_ref, out_hbm, out_ref, sems):
    lg = lg_ref[...]
    copies = []
    for i in range(2):
        at = pl.ds(i * 1024, 1024)
        part = dot(lg, near_ref[TOK:, at], 0, 0)
        out_ref[:, at] = (near_ref[:TOK, at].astype(F32) + part).astype(BF16)
        copies.append(pltpu.make_async_copy(out_ref.at[:, at], out_hbm.at[:, at], sems.at[i]))
        copies[i].start()
    for copy in copies:
        copy.wait()


def router_kernel(
    s_ref, code_ref, gate_ref, recv_ref, tie_ref, out_ref, cols_ref, spread_ref, lg_ref
):
    del tie_ref
    spread_ref[...] = spreading()
    for g in range(GROUPS):
        cols = [recv_ref[4 * g + i, ROWS:, :128].astype(F32) for i in range(4)]
        for h in range(4):
            cols_ref[h * 8 : (h + 1) * 8, g * 128 : (g + 1) * 128] = gather(cols, h)
    lane = iota((PEERS, 128), 1)
    tiles = [s_ref[pl.ds(t, PEERS, stride=3), :] for t in range(3)]
    for g in range(GROUPS):
        t, offset = g * 24 // 128, g * 24 % 128
        x = pltpu.roll(tiles[t], 128 - offset, axis=1) if offset else tiles[t]
        if offset + 24 > 128:
            x = jnp.where(lane < 128 - offset, x, pltpu.roll(tiles[t + 1], 128 - offset, axis=1))
        x = jnp.where(lane < 24, x, 0.0)
        hi = x.astype(BF16).astype(F32)
        rest = x - hi
        mid = rest.astype(BF16).astype(F32)
        low = (rest - mid).astype(BF16).astype(F32)
        z = hi + pltpu.roll(mid, 32, axis=1) + pltpu.roll(low, 64, axis=1)
        wide = dot(z.astype(BF16), spread_ref[...], 1, 0)
        code = code_ref[g].astype(F32)
        sdg = jnp.zeros((PEERS, 128), F32)
        for c in range(CAP):
            sdg = jnp.where(code == c, wide[:, c * 128 : (c + 1) * 128], sdg)
        total = jnp.sum(sdg, axis=0, keepdims=True)
        lg_ref[:, g * 128 : (g + 1) * 128] = (sdg - gate_ref[g].astype(F32) * total).astype(BF16)
    out_ref[...] = dot(cols_ref[...].astype(BF16), lg_ref[...], 1, 1)


def call(kernel, outs, scratch=(), flops=0, moved=0, **kw):
    return pl.pallas_call(
        kernel,
        out_shape=outs,
        scratch_shapes=list(scratch),
        compiler_params=pltpu.CompilerParams(vmem_limit_bytes=kw.pop("limit", 32) << 20),
        cost_estimate=pl.CostEstimate(flops=flops, bytes_accessed=moved, transcendentals=0),
        **kw,
    )


def whole():
    return pl.BlockSpec(memory_space=pltpu.VMEM)


def far():
    return pl.BlockSpec(memory_space=pltpu.HBM)


def struct(shape, dtype):
    return jax.ShapeDtypeStruct(shape, dtype)


def pack(og, li, rw, ids):
    return call(
        pack_kernel,
        (struct((PEERS, CHUNK, WIDE), BF16), struct((TOK + PEERS, PARTS * WIDE), BF16)),
        [pltpu.VMEM(a.shape, a.dtype) for a in (og, li, rw, ids)]
        + [pltpu.VMEM((PEERS, WIDE), F32)] * 2
        + [pltpu.SemaphoreType.DMA((6,))],
        flops=10**9,
        moved=2 * 10**6,
        in_specs=[far()] * 4,
        out_specs=(whole(), far()),
        name="pack",
    )(og, li, rw, ids)


def expert(recv, w, h, perm):
    return call(
        expert_kernel,
        (struct((SLOTS, SLOTS), BF16), struct((PEERS * 3, 128), F32)),
        [pltpu.VMEM((SLOTS, PARTS * WIDE), BF16)],
        flops=12 * 10**8,
        moved=4 * 10**6,
        name="expert",
    )(recv, w, h, perm)


def side(recv, hg):
    return call(
        side_kernel,
        (
            struct((GROUPS, PEERS, 128), BF16),
            struct((GROUPS, PEERS, 128), BF16),
            struct(hg.shape, BF16),
        ),
        [pltpu.SemaphoreType.DMA],
        flops=10**8,
        moved=2 * 10**6,
        out_specs=(whole(), whole(), far()),
        name="side",
    )(recv, hg)


def logit_grads(me, s, code, gate):
    return call(
        logit_kernel,
        struct((PEERS, TOK), BF16),
        flops=10**6,
        moved=2 * 10**5,
        in_specs=[pl.BlockSpec(memory_space=pltpu.SMEM)] + [whole()] * 3,
        name="logits",
    )(me, s, code, gate)


def input_grads(lg, near):
    shape = (TOK, PARTS * WIDE)
    return call(
        input_kernel,
        struct(shape, BF16),
        [pltpu.VMEM(shape, BF16), pltpu.SemaphoreType.DMA((2,))],
        flops=10**7,
        moved=10**6,
        out_specs=far(),
        name="inputs",
    )(lg, near)


def router_grads(s, code, gate, recv, tie):
    return call(
        router_kernel,
        struct((TOK, PEERS), F32),
        [
            pltpu.VMEM((TOK, PEERS * TOK), F32),
            pltpu.VMEM((128, CAP * 128), BF16),
            pltpu.VMEM((PEERS, PEERS * TOK), BF16),
        ],
        flops=40 * 10**8,
        moved=2 * 10**6,
        name="router",
    )(s, code, gate, recv, tie)


def shifted(x):
    n = lax.axis_size("section")
    return lax.ppermute(x, "section", [(i, (i - 1) % n) for i in range(n)])


def exchange(x):
    return lax.all_to_all(x, "expert", split_axis=0, concat_axis=0, tiled=True)


def shards(out_grad, layer_input, router_weight, expert_ids, hidden_act, down_weight):
    og, li = out_grad[0], layer_input[0]
    rw = jnp.swapaxes(router_weight[0], 0, 1)
    ids = jnp.swapaxes(expert_ids[0], 0, 1)
    far_args = [pltpu.with_memory_space_constraint(a, pltpu.HBM) for a in (og, li, rw, ids)]
    me = lax.axis_index("expert").astype(jnp.int32).reshape(1)
    send, near = pack(*far_args)
    recv = exchange(send)
    hidden_near, sdg = expert(
        recv, down_weight[0, 0], hidden_act[0, 0], jnp.asarray(compaction(), BF16)
    )
    back = exchange(sdg.reshape(PEERS, 1, SLOTS)).reshape(PEERS * 3, 128)
    near_next = shifted(near)
    all_gate, all_code, hidden_grad = side(recv, hidden_near)
    logit_grad = logit_grads(me, back, all_code, all_gate)
    logit_next = shifted(logit_grad)
    router_grad = router_grads(back, all_code, all_gate, recv, logit_grad)
    sent = input_grads(logit_next, near_next)[None]
    return sent, hidden_grad[None, None], router_grad[None]


def solution(mesh):
    placed = (
        P("section", "expert", None),
        P("section", "expert", None),
        P("section", None, None),
        P("section", "expert", None),
        P("section", "expert", None, None),
        P("section", "expert", None, None),
    )
    return jax.shard_map(
        shards,
        mesh=mesh,
        in_specs=placed,
        out_specs=(
            P("section", "expert", None),
            P("section", "expert", None, None),
            P("section", "expert", None),
        ),
        check_vma=False,
    )
```
